32 devices in a mesh: cam: 2 (over y), tm: 16 (over z, x, core).
Axes of the slice: x: 2, y: 2, z: 4, core: 2. Of those that a mesh axis runs over, the one named last changes fastest.
Arguments:
- keypoints: int32 [4, 34, 8192], P('cam', None, 'tm'), may hold values from 0 to 4095
- visibility: int32 [4, 8192], P(None, 'tm'), may hold values 0 or 1
- expand_weight: bfloat16 [3, 34, 1024], replicated, may hold values from -0.625 to 0.625
- dilated_tap_weight: bfloat16 [1024, 3, 1024], P('tm'), may hold values from -0.109375 to 0.109375
- join_weight: bfloat16 [1024, 64], replicated, may hold values from -0.1875 to 0.1875
- decay_rates: float32 [64, 8192], P('cam', 'tm'), may hold values from 0 to 1, as said below
Outputs:
- smoothed: float32 [64, 8192], P('cam', 'tm')
The draws below stay inside these ranges and needn't reach their ends.
Inputs may be any that keep to these rules, and one draw needn't show every extreme that they name: `keypoints`: quantized image coordinates. `decay_rates`: positive rates.
All inputs are finite; a program needn't handle non-finite values. No bound on the sum of `visibility` on one device may be relied on, other than what follows from the above.
Results may differ from the reference program's by a relative error of at most 0.00045.
Values may be sent and summed in bfloat16 or wider, within the bound.
A program may use at most 64 MiB of HBM per device.

```python
import jax
import jax.numpy as jnp
from jax import lax

C = 1024
J2 = 34
STATE = 64
DILATION_STEP = 3
FR_DEV = 512
CAMERAS = 4
CLIP_LENGTH = 8192


def draw_decay_rates(key, part):
    keys = jax.random.split(key, 7)
    slow_flag = jax.random.randint(keys[0], (STATE, 1), 0, 2) == 1
    fast_rate = jnp.exp(jax.random.uniform(keys[1], (STATE, 1), jnp.float32, jnp.log(1.0 / 50.0), jnp.log(1.0 / 30.0)))
    slow_rate = jnp.exp(jax.random.uniform(keys[2], (STATE, 1), jnp.float32, jnp.log(0.05), jnp.log(0.4))) / CLIP_LENGTH
    reference_decay_speed = jnp.where(slow_flag, slow_rate, fast_rate)
    interval_multiplier = jnp.exp(jax.random.uniform(keys[3], (STATE, CLIP_LENGTH // FR_DEV), jnp.float32, jnp.log(0.5), jnp.log(2.0)))
    interval_multiplier = jnp.repeat(interval_multiplier, FR_DEV, axis=1)
    instant_multiplier = jnp.exp(jax.random.uniform(keys[4], (STATE, CLIP_LENGTH), jnp.float32, jnp.log(0.5), jnp.log(2.0)))
    marker_locations = jax.random.randint(keys[5], (2,), 0, CLIP_LENGTH)
    retain_flags = jax.random.uniform(keys[6], (2,), jnp.float32, 0.5, 0.8)
    moment_number = jnp.arange(CLIP_LENGTH)
    spike_trace = jnp.zeros((CLIP_LENGTH,), jnp.float32)
    for chosen_location in range(2):
        spike_trace = spike_trace + jnp.where(moment_number == marker_locations[chosen_location], -jnp.log(retain_flags[chosen_location]), 0.0)
    return (reference_decay_speed * interval_multiplier * instant_multiplier + spike_trace[None, :]).astype(jnp.float32)


def place_ends(result, stream_key, low, high):
    index_at = [jax.random.randint(jax.random.fold_in(stream_key, axis), (), 0, length) for axis, length in enumerate(result.shape)]
    longest = result.shape.index(max(result.shape))
    next_to = index_at[:longest] + [(index_at[longest] + 1) % result.shape[longest]] + index_at[longest + 1:]
    return result.at[tuple(index_at)].set(low).at[tuple(next_to)].set(high)


def shard_levels(own_key, extent, cuts, low, top_value):
    loudness, own = 1.0, jax.random.fold_in(own_key, 6)
    for position, blocks in cuts:
        heights = jnp.exp(jax.random.uniform(jax.random.fold_in(own, position), (blocks,), jnp.float32, low / len(cuts), top_value / len(cuts)))
        loudness = loudness * jnp.repeat(heights, extent[position] // blocks).reshape([-1 if axis == position else 1 for axis in range(len(extent))])
    return loudness


def normal_values(rng, extent, deviation, most, pieces=(), dtype=jnp.bfloat16):
    result = deviation * jax.random.normal(rng, extent, jnp.float32)
    if pieces:
        result = result * shard_levels(rng, extent, pieces, -0.22, 0.18)
    return jnp.clip(result, -most, most).astype(dtype)


def setup_inputs(seed: int = 0) -> dict:
    key_list = jax.random.split(jax.random.key(seed), 7)
    keypoints = place_ends(jax.random.randint(key_list[0], (CAMERAS, J2, CLIP_LENGTH), 0, 4096), jax.random.fold_in(key_list[0], 1), 0, 4095).astype(jnp.int32)
    visibility = place_ends((jax.random.randint(key_list[1], (CAMERAS, CLIP_LENGTH), 0, 4) < 1).astype(jnp.int32), jax.random.fold_in(key_list[1], 1), 0, 1)
    expand_weight = normal_values(key_list[2], (3, J2, C), (3 * J2) ** -0.5, 0.625)
    dilated_tap_weight = normal_values(key_list[3], (C, 3, C), (3 * C) ** -0.5, 0.109375, ((0, 16),))
    join_weight = normal_values(key_list[4], (C, STATE), C ** -0.5, 0.1875)
    decay_rates = draw_decay_rates(jax.random.fold_in(key_list[6], 71), 0)
    return dict(keypoints=keypoints, visibility=visibility, expand_weight=expand_weight, dilated_tap_weight=dilated_tap_weight, join_weight=join_weight, decay_rates=decay_rates)


def reference(keypoints, visibility, expand_weight, dilated_tap_weight, join_weight, decay_rates):
    count_of_frames = keypoints.shape[2]

    def one_view(inputs):
        codes, seen_row = inputs
        coords = ((codes.astype(jnp.float32) - 2048.0) / 2048.0).astype(jnp.bfloat16)
        padded_input = jnp.pad(coords, ((0, 0), (1, 1)))
        first = jnp.zeros((count_of_frames, C), jnp.float32)
        for shift_amount in range(3):
            first = first + jnp.dot(padded_input[:, shift_amount:shift_amount + count_of_frames].T, expand_weight[shift_amount], preferred_element_type=jnp.float32)
        hidden_start0 = jax.nn.relu(first).astype(jnp.bfloat16)
        widened_output = jnp.pad(hidden_start0, ((DILATION_STEP, DILATION_STEP), (0, 0)))
        mixed_features = jnp.zeros((count_of_frames, C), jnp.float32)
        for shift_amount in range(3):
            mixed_features = mixed_features + jnp.dot(widened_output[shift_amount * DILATION_STEP:shift_amount * DILATION_STEP + count_of_frames], dilated_tap_weight[:, shift_amount, :].T, preferred_element_type=jnp.float32)
        hidden1 = (hidden_start0.astype(jnp.float32) + jax.nn.relu(mixed_features)).astype(jnp.bfloat16)
        projected = jnp.dot(hidden1, join_weight, preferred_element_type=jnp.float32)
        return (projected * seen_row.astype(jnp.float32)[:, None]).T
    terms = lax.map(one_view, (keypoints, visibility))
    total = lax.optimization_barrier(jnp.sum(terms, axis=0))
    seen = lax.optimization_barrier(jnp.sum(visibility.astype(jnp.float32), axis=0))
    joined = total / jnp.maximum(seen, 1.0)[None, :]
    decay = jnp.exp(-decay_rates)
    energy = -jnp.expm1(-2.0 * decay_rates)
    drive = jnp.sqrt(energy)

    def forward_step(state, inputs):
        factor, gain, value = inputs
        state = factor * state + gain * value
        return (state, state)
    start = jnp.zeros((decay_rates.shape[0],), jnp.float32)
    _, filtered = lax.scan(forward_step, start, (decay.T, drive.T, joined.T))

    def backward_step(state, inputs):
        factor, weight, value = inputs
        state = factor * state + weight * value
        return (state, state)
    _, smoothed = lax.scan(backward_step, start, (decay.T, energy.T, filtered), reverse=True)
    return smoothed.T
```

```python
import functools

import jax
import jax.numpy as jnp
from jax import lax
from jax.experimental import pallas as pl
from jax.experimental.pallas import tpu as pltpu
from jax.sharding import PartitionSpec as P

DILATION_STEP = 3
MESH = pl.DeviceIdType.MESH


def with_halo(array, sides, width):
    for axis, dim in sides:
        count, length = (lax.axis_size(axis), array.shape[dim])
        up = [(i, (i + 1) % count) for i in range(count - 1)]
        down = [(j, i) for i, j in up]
        last = lax.slice_in_dim(array, length - width, length, axis=dim)
        initial = lax.slice_in_dim(array, 0, width, axis=dim)
        before = lax.ppermute(last, axis, up)
        after = lax.ppermute(initial, axis, down)
        array = jnp.concatenate([before, array, after], axis=dim)
    return array


def entering(part, axis, combine, identity, reverse):
    count = lax.axis_size(axis)
    place = lax.axis_index(axis)
    ahead = count - 1 - place if reverse else place
    gathered = jax.tree.map(lambda a: lax.all_gather(a, axis), part)
    state = jax.tree.map(lambda a, e: jnp.zeros_like(a) + jnp.asarray(e, a.dtype), part, identity)

    def one(turn, state):
        source = count - 1 - turn if reverse else turn
        return combine(
            state, jax.tree.map(lambda a: lax.dynamic_index_in_dim(a, source, 0, False), gathered)
        )

    return lax.fori_loop(0, ahead, one, state)


def expand(widened_output, expand_weight, width):
    total = None
    for shift_amount in range(3):
        term = jnp.einsum(
            "vjt,jc->vtc",
            widened_output[:, :, shift_amount : shift_amount + width],
            expand_weight[shift_amount],
            preferred_element_type=jnp.float32,
        )
        total = term if total is None else total + term
    return jax.nn.relu(total).astype(jnp.bfloat16)


def dilate(padded_input, hidden_start0, weight_rows):
    count_of_frames = hidden_start0.shape[1]
    total = None
    for shift_amount in range(3):
        term = jnp.einsum(
            "vti,ni->vtn",
            padded_input[
                :, shift_amount * DILATION_STEP : shift_amount * DILATION_STEP + count_of_frames
            ],
            weight_rows[:, shift_amount],
            preferred_element_type=jnp.float32,
        )
        total = term if total is None else total + term
    residual = hidden_start0.astype(jnp.float32)
    return (residual + jax.nn.relu(total)).astype(jnp.bfloat16)


def chain(earlier, latter):
    return (earlier[0] * latter[0], latter[0] * earlier[1] + latter[1])


def body(keypoints, visibility, expand_weight, dilated_tap_weight, join_weight, decay_rates):
    view_count = keypoints.shape[0]
    count_of_frames = keypoints.shape[2]
    coords = ((keypoints.astype(jnp.float32) - 2048.0) / 2048.0).astype(jnp.bfloat16)
    widened_output = with_halo(coords, (("tm", 2),), 1)
    hidden_start0 = expand(widened_output, expand_weight, count_of_frames)
    padded_input = with_halo(hidden_start0, (("tm", 1),), DILATION_STEP)
    hidden1 = dilate(
        padded_input, hidden_start0, lax.all_gather(dilated_tap_weight, "tm", axis=0, tiled=True)
    )
    own_mask = lax.dynamic_slice_in_dim(
        visibility, lax.axis_index("cam") * view_count, view_count, 0
    )
    masked = hidden1 * own_mask[:, :, None].astype(jnp.bfloat16)
    state_rows = decay_rates.shape[0]
    total = lax.psum_scatter(
        jnp.einsum("vti,is->st", masked, join_weight, preferred_element_type=jnp.float32).astype(
            jnp.bfloat16
        ),
        "cam",
        scatter_dimension=0,
        tiled=True,
    ).astype(jnp.float32)
    seen = jnp.sum(visibility.astype(jnp.float32), axis=0)
    joined = total / jnp.maximum(seen, 1.0)[None, :]
    decay = jnp.exp(-decay_rates)
    energy = -jnp.expm1(-2.0 * decay_rates)
    drive = jnp.sqrt(energy)
    prod_fwd, local_fwd = lax.associative_scan(chain, (decay, drive * joined), axis=1)
    ones_vec = jnp.ones((state_rows,), jnp.float32)
    zeros_vec = jnp.zeros((state_rows,), jnp.float32)
    carried = entering(
        (prod_fwd[:, -1], local_fwd[:, -1]), "tm", chain, (ones_vec, zeros_vec), False
    )
    filtered = local_fwd + prod_fwd * carried[1][:, None]
    prod_back, local_back = lax.associative_scan(
        chain, (decay, energy * filtered), axis=1, reverse=True
    )
    returned = entering(
        (prod_back[:, 0], local_back[:, 0]), "tm", chain, (ones_vec, zeros_vec), True
    )
    smoothed = local_back + prod_back * returned[1][:, None]
    return smoothed

SIDE = 128
DEPTH = 48
LANES = 128


def neg_expm1(u):
    series = jnp.ones_like(u)
    for k in range(11, 1, -1):
        series = 1.0 - series * u * (1.0 / k)
    return jnp.where(u < 0.5, u * series, 1.0 - jnp.exp(-u))


def block_kernel(
    cams, layers, group, keys_ref, vis_ref, first_ref, taps_ref, join_ref, rates_ref, out_ref,
    coords, hidden, mixed, weights, stage, part_out, part_in, ends,
    coord_send, coord_recv, side_send, side_recv, up_send, down_send, tap_recv,
    part_send, part_recv, end_send, end_recv,
):
    views, joints, length = keys_ref.shape
    channels = first_ref.shape[0]
    count = layers * group
    all_cams = cams * views
    rows = taps_ref.shape[1] // cams
    own = layers * rows
    states = rates_ref.shape[0]
    all_states = join_ref.shape[1]
    members = group * cams
    span = group * length
    f32, bf16 = jnp.float32, jnp.bfloat16
    y = lax.axis_index("cam")
    i = lax.axis_index("tm")
    z = i // group
    l = i % group
    me = l * cams + y

    barrier = pltpu.get_barrier_semaphore()
    everyone = cams * count
    flat = i * cams + y

    @pl.loop(1, everyone)
    def _(d):
        other = lax.rem(flat + d, everyone)
        pl.semaphore_signal(
            barrier, inc=1, device_id=(other % cams, other // cams), device_id_type=MESH
        )

    here = pl.ds(pl.multiple_of(SIDE + l * length, LANES), length)
    for v in range(views):
        stage[...] = jnp.zeros_like(stage)
        stage[pl.ds(0, joints), :] = (keys_ref[v].astype(f32) - 2048.0) / 2048.0
        stage[pl.ds(joints, 1), :] = vis_ref[pl.ds(y * views + v, 1), :].astype(f32)
        coords[y * views + v, :, here] = stage[...].astype(bf16)

    @pl.when(z == 0)
    def _():
        coords[:, :, 0:SIDE] = jnp.zeros((all_cams, DEPTH, SIDE), bf16)

    @pl.when(z == layers - 1)
    def _():
        coords[:, :, SIDE + span : SIDE + span + SIDE] = jnp.zeros((all_cams, DEPTH, SIDE), bf16)

    pl.semaphore_wait(barrier, everyone - 1)

    def tap_copy(source, target, sem, first):
        src = taps_ref.at[:, pl.ds(pl.multiple_of(y * rows, rows), rows), :]
        if not first:
            src = weights.at[pl.ds(0, 3), source]
        return pltpu.make_async_remote_copy(
            src_ref=src,
            dst_ref=weights.at[pl.ds(0, 3), source],
            send_sem=sem.at[source],
            recv_sem=tap_recv.at[source],
            device_id=(y, target * group + l),
            device_id_type=MESH,
        )

    def pass_on(source, upward, first):
        if upward:
            @pl.when(z < layers - 1)
            def _():
                tap_copy(source, z + 1, up_send, first).start()
        else:
            @pl.when(z > 0)
            def _():
                tap_copy(source, z - 1, down_send, first).start()

    def arrive(hop):
        @pl.when(z >= hop)
        def _():
            tap_copy(z - hop, z, up_send, False).wait_recv()
            if hop < layers - 1:
                pass_on(z - hop, True, False)

        @pl.when(z + hop < layers)
        def _():
            tap_copy(z + hop, z, down_send, False).wait_recv()
            if hop < layers - 1:
                pass_on(z + hop, False, False)

    def side_copy(side, sender, target, sem):
        cam_rows = pl.ds(sender * views, views)
        if side == 0:
            src, dst = pl.ds(span, SIDE), pl.ds(0, SIDE)
        else:
            src, dst = pl.ds(SIDE, SIDE), pl.ds(SIDE + span, SIDE)
        return pltpu.make_async_remote_copy(
            src_ref=coords.at[cam_rows, :, src],
            dst_ref=coords.at[cam_rows, :, dst],
            send_sem=sem,
            recv_sem=side_recv.at[side * cams + sender],
            device_id=target,
            device_id_type=MESH,
        )

    def coord_copy(sender, target, sem):
        lanes = pl.ds(pl.multiple_of(SIDE + (sender // cams) * length, LANES), length)
        at = coords.at[pl.ds((sender % cams) * views, views), :, lanes]
        return pltpu.make_async_remote_copy(
            src_ref=at,
            dst_ref=at,
            send_sem=sem,
            recv_sem=coord_recv.at[sender],
            device_id=(target % cams, z * group + target // cams),
            device_id_type=MESH,
        )

    pass_on(z, True, True)
    pass_on(z, False, True)

    for d in range(1, members):
        target = lax.rem(me + d, members)
        coord_copy(me, target, coord_send.at[target]).start()

    @pl.when((l == group - 1) & (z < layers - 1))
    def _():
        for p in range(members):
            side_copy(0, y, (p % cams, (z + 1) * group + p // cams), side_send.at[p]).start()

    @pl.when((l == 0) & (z > 0))
    def _():
        for p in range(members):
            side_copy(1, y, (p % cams, (z - 1) * group + p // cams), side_send.at[p]).start()

    for o in range(3):
        weights[o, z] = taps_ref[o, pl.ds(pl.multiple_of(y * rows, rows), rows), :]
    for s in range(layers):
        base = (s * group + l) * (rows * cams) + y * rows
        r = lax.broadcasted_iota(jnp.int32, (rows, channels), 0)
        c = lax.broadcasted_iota(jnp.int32, (rows, channels), 1)
        weights[3, s] = jnp.where(c == r + base, 1.0, 0.0).astype(bf16)

    lane = lax.broadcasted_iota(jnp.int32, (states, length), 1)

    def scan(prod, values, reverse):
        step = 1
        while step < length:
            turn = length - step if reverse else step
            fits = (lane < length - step) if reverse else (lane >= step)
            values = [
                val + prod * jnp.where(fits, pltpu.roll(val, turn, 1), 0.0) for val in values
            ]
            prod = prod * jnp.where(fits, pltpu.roll(prod, turn, 1), 1.0)
            step *= 2
        return prod, values

    for d in range(1, members):
        source = lax.rem(me + members - d, members)
        coord_copy(source, source, coord_send.at[source]).wait_recv()

    @pl.when(z > 0)
    def _():
        for p in range(cams):
            side_copy(0, p, (y, i), side_send.at[p]).wait_recv()

    @pl.when(z < layers - 1)
    def _():
        for p in range(cams):
            side_copy(1, p, (y, i), side_send.at[p]).wait_recv()

    def expand_block(v, start, width):
        wide = coords[v, :, pl.ds(start - SIDE, width + 2 * SIDE)].astype(f32)
        full = width + 2 * SIDE
        x = jnp.concatenate(
            [
                pltpu.roll(wide, 1, 1)[:, SIDE : SIDE + width],
                wide[:, SIDE : SIDE + width],
                pltpu.roll(wide, full - 1, 1)[:, SIDE : SIDE + width],
            ],
            axis=0,
        ).astype(bf16)
        return jnp.maximum(jnp.dot(first_ref[...], x, preferred_element_type=f32), 0.0)

    def expand_some(begin, end):
        @pl.loop(begin, end)
        def _(n):
            v, s = n // group, n % group
            start = pl.multiple_of(SIDE + s * length, LANES)
            hidden[n] = expand_block(v, start, length).astype(bf16)

    whole = all_cams * group
    expand_some(0, whole // 4)
    arrive(1)
    expand_some(whole // 4, whole // 2)
    for hop in range(2, layers - 1):
        arrive(hop)
    expand_some(whole // 2, whole)

    slab = lax.broadcasted_iota(jnp.int32, (DEPTH, SIDE), 1)
    low = slab < SIDE // 2
    wide_slab = lax.broadcasted_iota(jnp.int32, (channels, SIDE), 1)
    keep = ((wide_slab < SIDE // 2) & (z < layers - 1)) | ((wide_slab >= SIDE // 2) & (z > 0))
    for v in range(all_cams):
        before = coords[v, :, 0:SIDE].astype(f32)
        begin = coords[v, :, SIDE : 2 * SIDE].astype(f32)
        end = coords[v, :, span : SIDE + span].astype(f32)
        after = coords[v, :, SIDE + span : SIDE + span + SIDE].astype(f32)
        older = jnp.where(slab == 0, pltpu.roll(end, 1, 1), pltpu.roll(after, 1, 1))
        newer = jnp.where(
            slab == SIDE - 1, pltpu.roll(begin, SIDE - 1, 1), pltpu.roll(before, SIDE - 1, 1)
        )
        x = jnp.concatenate(
            [
                jnp.where(low, older, pltpu.roll(before, 1, 1)),
                jnp.where(low, after, before),
                jnp.where(low, pltpu.roll(after, SIDE - 1, 1), newer),
            ],
            axis=0,
        ).astype(bf16)
        h = jnp.maximum(jnp.dot(first_ref[...], x, preferred_element_type=f32), 0.0)
        hidden[whole, :, v * SIDE : (v + 1) * SIDE] = jnp.where(keep, h, 0.0).astype(bf16)

    rates = rates_ref[...]
    decay = jnp.exp(-rates)
    energy = neg_expm1(2.0 * rates)
    drive = jnp.sqrt(energy)

    arrive(layers - 1)
    stack = weights[...].reshape(4 * own, channels)

    z_slab = jnp.dot(stack, hidden[whole], preferred_element_type=f32)
    for v in range(all_cams):
        piece = z_slab[:, v * SIDE : (v + 1) * SIDE]
        mixed[v, :, 0:SIDE] = piece
        mixed[v, :, SIDE + span : SIDE + span + SIDE] = piece

    @pl.loop(0, whole)
    def _(n):
        v, s = n // group, n % group
        lanes = pl.ds(pl.multiple_of(SIDE + s * length, LANES), length)
        mixed[v, :, lanes] = jnp.dot(
            weights[...].reshape(4 * own, channels), hidden[n], preferred_element_type=f32
        )

    picked = jnp.concatenate(
        [
            join_ref[pl.ds(pl.multiple_of((s * group + l) * (rows * cams) + y * rows, rows), rows), :]
            for s in range(layers)
        ],
        axis=0,
    )
    twice = jnp.concatenate([picked, picked], axis=0)

    def part_copy(slot, source, target, sem):
        return pltpu.make_async_remote_copy(
            src_ref=part_out.at[slot],
            dst_ref=part_in.at[source],
            send_sem=sem,
            recv_sem=part_recv.at[source],
            device_id=(target % cams, z * group + target // cams),
            device_id_type=MESH,
        )

    for d in range(group):
        s = lax.rem(l + d + 1, group)
        centre = pl.ds(pl.multiple_of(SIDE + s * length, LANES), length)
        earlier = pl.ds(pl.multiple_of(s * length, LANES), SIDE + length)
        later = pl.ds(pl.multiple_of(SIDE + s * length, LANES), SIDE + length)
        total = jnp.zeros((own, length), f32)
        for v in range(all_cams):
            left = pltpu.roll(mixed[v, 0:own, earlier], DILATION_STEP, 1)[:, SIDE:]
            right = pltpu.roll(
                mixed[v, 2 * own : 3 * own, later], SIDE + length - DILATION_STEP, 1
            )[:, :length]
            acc = left + mixed[v, own : 2 * own, centre] + right
            h = (mixed[v, 3 * own : 4 * own, centre] + jnp.maximum(acc, 0.0)).astype(bf16)
            mask = coords[v, :, centre].astype(f32)[joints : joints + 1, :]
            total = total + h.astype(f32) * mask
        top = total.astype(bf16)
        rest = (total - top.astype(f32)).astype(bf16)
        both = jnp.concatenate([top, rest], axis=0)
        result = lax.dot_general(
            twice, both, (((0,), (0,)), ((), ())), preferred_element_type=f32
        ).astype(bf16)
        for p in range(cams):
            part_out[s * cams + p] = result[p * states : (p + 1) * states]
        for p in range(cams):
            target = s * cams + p
            if d < group - 1:
                part_copy(target, me, target, part_send.at[target]).start()
            else:
                @pl.when(p != y)
                def _():
                    part_copy(target, me, target, part_send.at[target]).start()

                @pl.when(p == y)
                def _():
                    part_in[me] = part_out[target]

    seen = jnp.sum(vis_ref[...].astype(f32), axis=0, keepdims=True)
    for d in range(1, members):
        source = lax.rem(me + members - d, members)
        part_copy(source, source, source, part_send.at[source]).wait_recv()
    summed = part_in[0].astype(f32)
    for p in range(1, members):
        summed = summed + part_in[p].astype(f32)
    joined = summed / jnp.maximum(seen, 1.0)

    prod_fwd, (local,) = scan(decay, [drive * joined], False)
    prod_back, (back, through) = scan(decay, [energy * local, energy * prod_fwd], True)

    square = lax.broadcasted_iota(jnp.int32, (states, LANES), 1)
    packed = jnp.where(
        square == 0,
        prod_fwd[:, length - 1 : length],
        jnp.where(
            square == 1,
            local[:, length - 1 : length],
            jnp.where(square == 2, back[:, 0:1], through[:, 0:1]),
        ),
    )
    packed = jnp.concatenate([packed, jnp.zeros((LANES - states, LANES), f32)], axis=0)
    ends[i] = packed.T[0:8]

    def end_copy(source, target, sem):
        return pltpu.make_async_remote_copy(
            src_ref=ends.at[source],
            dst_ref=ends.at[source],
            send_sem=sem,
            recv_sem=end_recv.at[source],
            device_id=(y, target),
            device_id_type=MESH,
        )

    for d in range(1, count):
        target = lax.rem(i + d, count)
        end_copy(i, target, end_send.at[target]).start()
    for d in range(1, count):
        source = lax.rem(i + count - d, count)
        end_copy(source, source, end_send.at[source]).wait_recv()

    entry = jnp.zeros((1, LANES), f32)
    carried = entry
    entries = []
    for j in range(count):
        entries.append(entry)
        carried = jnp.where(j == i, entry, carried)
        entry = ends[j, 0:1] * entry + ends[j, 1:2]
    state = jnp.zeros((1, LANES), f32)
    returned = state
    for j in range(count - 1, -1, -1):
        returned = jnp.where(j == i, state, returned)
        state = ends[j, 0:1] * state + ends[j, 2:3] + ends[j, 3:4] * entries[j]
    both = jnp.concatenate([carried, returned, jnp.zeros((LANES - 2, LANES), f32)], axis=0).T
    out_ref[...] = back + through * both[0:states, 0:1] + prod_back * both[0:states, 1:2]

    for d in range(1, members):
        target = lax.rem(me + d, members)
        coord_copy(me, target, coord_send.at[target]).wait_send()
        part_copy(target, me, target, part_send.at[target]).wait_send()
    for d in range(1, count):
        target = lax.rem(i + d, count)
        end_copy(i, target, end_send.at[target]).wait_send()

    @pl.when((l == group - 1) & (z < layers - 1))
    def _():
        for p in range(members):
            side_copy(0, y, (p % cams, (z + 1) * group + p // cams), side_send.at[p]).wait_send()

    @pl.when((l == 0) & (z > 0))
    def _():
        for p in range(members):
            side_copy(1, y, (p % cams, (z - 1) * group + p // cams), side_send.at[p]).wait_send()

    for hop in range(layers - 1):
        @pl.when((z < layers - 1) & (z - hop >= 0))
        def _():
            tap_copy(z - hop, z + 1, up_send, hop == 0).wait_send()

        @pl.when((z > 0) & (z + hop < layers))
        def _():
            tap_copy(z + hop, z - 1, down_send, hop == 0).wait_send()


def block_body(cams, count, group):
    layers = count // group

    def run(keypoints, visibility, expand_weight, dilated_tap_weight, join_weight, decay_rates):
        views, joints, length = keypoints.shape
        channels = expand_weight.shape[2]
        rows = dilated_tap_weight.shape[0] // cams
        own = layers * rows
        members = group * cams
        all_cams = cams * views
        states = decay_rates.shape[0]
        first = jnp.pad(expand_weight, ((0, 0), (0, DEPTH - joints), (0, 0)))
        first = first.reshape(3 * DEPTH, channels).T
        taps = jnp.transpose(dilated_tap_weight, (1, 0, 2))
        extended = group * length + 2 * SIDE
        dma, vmem, bf16 = (pltpu.SemaphoreType.DMA, pltpu.VMEM, jnp.bfloat16)
        return pl.pallas_call(
            functools.partial(block_kernel, cams, layers, group),
            out_shape=jax.ShapeDtypeStruct(decay_rates.shape, jnp.float32),
            in_specs=[pl.BlockSpec(memory_space=pltpu.VMEM)] * 6,
            out_specs=pl.BlockSpec(memory_space=pltpu.VMEM),
            scratch_shapes=[
                vmem((all_cams, DEPTH, extended), bf16),
                vmem((all_cams * group + 1, channels, length), bf16),
                vmem((all_cams, 4 * own, extended), jnp.float32),
                vmem((4, layers, rows, channels), bf16),
                vmem((DEPTH, length), jnp.float32),
                vmem((members, states, length), bf16),
                vmem((members, states, length), bf16),
                vmem((count, 8, LANES), jnp.float32),
                dma((members,)),
                dma((members,)),
                dma((members,)),
                dma((2 * cams,)),
                dma((layers,)),
                dma((layers,)),
                dma((layers,)),
                dma((members,)),
                dma((members,)),
                dma((count,)),
                dma((count,)),
            ],
            compiler_params=pltpu.CompilerParams(
                collective_id=0, has_side_effects=True, vmem_limit_bytes=58 * 1024 * 1024
            ),
        )(keypoints, visibility, first, taps, join_weight, decay_rates)

    return run


def solution(mesh):
    cams, count = mesh.shape["cam"], mesh.shape["tm"]
    group = 4
    fits = count % group == 0 and cams == 2 and count == 4 * group
    return jax.shard_map(
        block_body(cams, count, group) if fits else body,
        mesh=mesh,
        in_specs=(
            P("cam", None, "tm"),
            P(None, "tm"),
            P(),
            P("tm", None, None),
            P(),
            P("cam", "tm"),
        ),
        out_specs=P("cam", "tm"),
        check_vma=False,
    )
```

```python
import functools

import jax
import jax.numpy as jnp
from jax import lax
from jax.experimental import pallas as pl
from jax.experimental.pallas import tpu as pltpu
from jax.sharding import PartitionSpec as P

DILATION_STEP = 3
MESH = pl.DeviceIdType.MESH


def with_halo(array, sides, width):
    for axis, dim in sides:
        count, length = (lax.axis_size(axis), array.shape[dim])
        up = [(i, (i + 1) % count) for i in range(count - 1)]
        down = [(j, i) for i, j in up]
        last = lax.slice_in_dim(array, length - width, length, axis=dim)
        initial = lax.slice_in_dim(array, 0, width, axis=dim)
        before = lax.ppermute(last, axis, up)
        after = lax.ppermute(initial, axis, down)
        array = jnp.concatenate([before, array, after], axis=dim)
    return array


def entering(part, axis, combine, identity, reverse):
    count = lax.axis_size(axis)
    place = lax.axis_index(axis)
    ahead = count - 1 - place if reverse else place
    gathered = jax.tree.map(lambda a: lax.all_gather(a, axis), part)
    state = jax.tree.map(lambda a, e: jnp.zeros_like(a) + jnp.asarray(e, a.dtype), part, identity)

    def one(turn, state):
        source = count - 1 - turn if reverse else turn
        return combine(
            state, jax.tree.map(lambda a: lax.dynamic_index_in_dim(a, source, 0, False), gathered)
        )

    return lax.fori_loop(0, ahead, one, state)


def expand(widened_output, expand_weight, width):
    total = None
    for shift_amount in range(3):
        term = jnp.einsum(
            "vjt,jc->vtc",
            widened_output[:, :, shift_amount : shift_amount + width],
            expand_weight[shift_amount],
            preferred_element_type=jnp.float32,
        )
        total = term if total is None else total + term
    return jax.nn.relu(total).astype(jnp.bfloat16)


def dilate(padded_input, hidden_start0, weight_rows):
    count_of_frames = hidden_start0.shape[1]
    total = None
    for shift_amount in range(3):
        term = jnp.einsum(
            "vti,ni->vtn",
            padded_input[
                :, shift_amount * DILATION_STEP : shift_amount * DILATION_STEP + count_of_frames
            ],
            weight_rows[:, shift_amount],
            preferred_element_type=jnp.float32,
        )
        total = term if total is None else total + term
    residual = hidden_start0.astype(jnp.float32)
    return (residual + jax.nn.relu(total)).astype(jnp.bfloat16)


def chain(earlier, latter):
    return (earlier[0] * latter[0], latter[0] * earlier[1] + latter[1])


def body(keypoints, visibility, expand_weight, dilated_tap_weight, join_weight, decay_rates):
    view_count = keypoints.shape[0]
    count_of_frames = keypoints.shape[2]
    coords = ((keypoints.astype(jnp.float32) - 2048.0) / 2048.0).astype(jnp.bfloat16)
    widened_output = with_halo(coords, (("tm", 2),), 1)
    hidden_start0 = expand(widened_output, expand_weight, count_of_frames)
    padded_input = with_halo(hidden_start0, (("tm", 1),), DILATION_STEP)
    hidden1 = dilate(
        padded_input, hidden_start0, lax.all_gather(dilated_tap_weight, "tm", axis=0, tiled=True)
    )
    own_mask = lax.dynamic_slice_in_dim(
        visibility, lax.axis_index("cam") * view_count, view_count, 0
    )
    masked = hidden1 * own_mask[:, :, None].astype(jnp.bfloat16)
    state_rows = decay_rates.shape[0]
    total = lax.psum_scatter(
        jnp.einsum("vti,is->st", masked, join_weight, preferred_element_type=jnp.float32).astype(
            jnp.bfloat16
        ),
        "cam",
        scatter_dimension=0,
        tiled=True,
    ).astype(jnp.float32)
    seen = jnp.sum(visibility.astype(jnp.float32), axis=0)
    joined = total / jnp.maximum(seen, 1.0)[None, :]
    decay = jnp.exp(-decay_rates)
    energy = -jnp.expm1(-2.0 * decay_rates)
    drive = jnp.sqrt(energy)
    prod_fwd, local_fwd = lax.associative_scan(chain, (decay, drive * joined), axis=1)
    ones_vec = jnp.ones((state_rows,), jnp.float32)
    zeros_vec = jnp.zeros((state_rows,), jnp.float32)
    carried = entering(
        (prod_fwd[:, -1], local_fwd[:, -1]), "tm", chain, (ones_vec, zeros_vec), False
    )
    filtered = local_fwd + prod_fwd * carried[1][:, None]
    prod_back, local_back = lax.associative_scan(
        chain, (decay, energy * filtered), axis=1, reverse=True
    )
    returned = entering(
        (prod_back[:, 0], local_back[:, 0]), "tm", chain, (ones_vec, zeros_vec), True
    )
    smoothed = local_back + prod_back * returned[1][:, None]
    return smoothed

SIDE = 128
DEPTH = 40
LANES = 128


def neg_expm1(u):
    series = jnp.ones_like(u)
    for k in range(11, 1, -1):
        series = 1.0 - series * u * (1.0 / k)
    return jnp.where(u < 0.5, u * series, 1.0 - jnp.exp(-u))


def block_kernel(
    cams, layers, group, keys_ref, vis_ref, raw_ref, taps_ref, join_ref, rates_ref, out_ref,
    first_wide, first_ref, coords, hidden, mixed, weights, stack, stage, part_out, part_in, ends,
    coord_send, coord_recv, relay_send, side_send, side_recv, up_send, down_send, tap_recv,
    part_send, part_recv, end_send, end_recv,
):
    joints, views, length = keys_ref.shape
    channels = raw_ref.shape[2]
    count = layers * group
    all_cams = cams * views
    rows = taps_ref.shape[1] // cams
    own = layers * rows
    states = rates_ref.shape[0]
    members = group * cams
    span = group * length
    f32, bf16 = jnp.float32, jnp.bfloat16
    y = lax.axis_index("cam")
    i = lax.axis_index("tm")
    z = i // group
    l = i % group
    me = l * cams + y

    barrier = pltpu.get_barrier_semaphore()
    everyone = cams * count
    flat = i * cams + y

    @pl.loop(1, everyone)
    def _(d):
        other = lax.rem(flat + d, everyone)
        pl.semaphore_signal(
            barrier, inc=1, device_id=(other % cams, other // cams), device_id_type=MESH
        )

    here = pl.ds(pl.multiple_of(SIDE + l * length, LANES), length)
    for v in range(views):
        stage[...] = jnp.zeros_like(stage)
        stage[pl.ds(0, joints), :] = (keys_ref[:, v, :].astype(f32) - 2048.0) / 2048.0
        stage[pl.ds(joints, 1), :] = vis_ref[pl.ds(y * views + v, 1), :].astype(f32)
        coords[y * views + v, :, here] = stage[...].astype(bf16)

    @pl.when(z == 0)
    def _():
        coords[:, :, 0:SIDE] = jnp.zeros((all_cams, DEPTH, SIDE), bf16)

    @pl.when(z == layers - 1)
    def _():
        coords[:, :, SIDE + span : SIDE + span + SIDE] = jnp.zeros((all_cams, DEPTH, SIDE), bf16)

    first_wide[...] = jnp.zeros_like(first_wide)
    for o in range(3):
        first_wide[pl.ds(o * DEPTH, joints), :] = raw_ref[o].astype(f32)
    first_ref[...] = first_wide[...].T[:, : 3 * DEPTH].astype(bf16)

    for o in range(3):
        weights[o, z] = taps_ref[o, pl.ds(pl.multiple_of(y * rows, rows), rows), :]
    for s in range(layers):
        base = (s * group + l) * (rows * cams) + y * rows
        r = lax.broadcasted_iota(jnp.int32, (rows, channels), 0)
        c = lax.broadcasted_iota(jnp.int32, (rows, channels), 1)
        weights[3, s] = jnp.where(c == r + base, 1.0, 0.0).astype(bf16)
    near = jnp.where(z < layers - 1, z + 1, z - 1)
    far = jnp.where(z == 0, 2, 0)
    last = jnp.where(z < 2, 3, 1)
    halves = ((z, near), (far, last))
    picked = lax.dot_general(
        join_ref[...],
        jnp.concatenate([weights[3, t] for pair in halves for t in pair], axis=0),
        (((1,), (1,)), ((), ())),
        preferred_element_type=f32,
    ).astype(bf16)
    twice = jnp.concatenate([picked, picked], axis=1)

    pl.semaphore_wait(barrier, everyone - 1)

    def tap_copy(source, target, sem, first):
        src = taps_ref.at[:, pl.ds(pl.multiple_of(y * rows, rows), rows), :]
        if not first:
            src = weights.at[pl.ds(0, 3), source]
        return pltpu.make_async_remote_copy(
            src_ref=src,
            dst_ref=weights.at[pl.ds(0, 3), source],
            send_sem=sem.at[source],
            recv_sem=tap_recv.at[source],
            device_id=(y, target * group + l),
            device_id_type=MESH,
        )

    def pass_on(source, upward, first):
        if upward:
            @pl.when(z < layers - 1)
            def _():
                tap_copy(source, z + 1, up_send, first).start()
        else:
            @pl.when(z > 0)
            def _():
                tap_copy(source, z - 1, down_send, first).start()

    def arrive(hop):
        @pl.when(z >= hop)
        def _():
            tap_copy(z - hop, z, up_send, False).wait_recv()
            if hop < layers - 1:
                pass_on(z - hop, True, False)

        @pl.when(z + hop < layers)
        def _():
            tap_copy(z + hop, z, down_send, False).wait_recv()
            if hop < layers - 1:
                pass_on(z + hop, False, False)

    def side_copy(side, sender, target, sem):
        cam_rows = pl.ds(sender * views, views)
        if side == 0:
            src, dst = pl.ds(span, SIDE), pl.ds(0, SIDE)
        else:
            src, dst = pl.ds(SIDE, SIDE), pl.ds(SIDE + span, SIDE)
        return pltpu.make_async_remote_copy(
            src_ref=coords.at[cam_rows, :, src],
            dst_ref=coords.at[cam_rows, :, dst],
            send_sem=sem,
            recv_sem=side_recv.at[side * cams + sender],
            device_id=target,
            device_id_type=MESH,
        )

    def coord_copy(sender, target, sem):
        lanes = pl.ds(pl.multiple_of(SIDE + (sender // cams) * length, LANES), length)
        at = coords.at[pl.ds((sender % cams) * views, views), :, lanes]
        return pltpu.make_async_remote_copy(
            src_ref=at,
            dst_ref=at,
            send_sem=sem,
            recv_sem=coord_recv.at[sender],
            device_id=(target % cams, z * group + target // cams),
            device_id_type=MESH,
        )

    pass_on(z, True, True)
    pass_on(z, False, True)

    turns = [(a, b) for a in range(group // 2) for b in range(cams) if a + b > 0]
    core = l % 2
    mate = (l + 1 - 2 * core) * cams + y

    def alike(a, b, side):
        chip = lax.rem(l // 2 + a, group // 2)
        return (chip * 2 + side) * cams + lax.rem(y + b, cams)

    coord_copy(me, mate, coord_send.at[mate]).start()
    for a, b in turns:
        target = alike(a, b, core)
        coord_copy(me, target, coord_send.at[target]).start()

    @pl.when((l == group - 1) & (z < layers - 1))
    def _():
        for p in range(members):
            side_copy(0, y, (p % cams, (z + 1) * group + p // cams), side_send.at[p]).start()

    @pl.when((l == 0) & (z > 0))
    def _():
        for p in range(members):
            side_copy(1, y, (p % cams, (z - 1) * group + p // cams), side_send.at[p]).start()

    lane = lax.broadcasted_iota(jnp.int32, (states, length), 1)

    def scan(prod, values, reverse):
        step = 1
        while step < length:
            turn = length - step if reverse else step
            fits = (lane < length - step) if reverse else (lane >= step)
            values = [
                val + prod * jnp.where(fits, pltpu.roll(val, turn, 1), 0.0) for val in values
            ]
            prod = prod * jnp.where(fits, pltpu.roll(prod, turn, 1), 1.0)
            step *= 2
        return prod, values

    for a, b in turns:
        source = alike(a, b, core)
        coord_copy(source, source, coord_send.at[source]).wait_recv()
        coord_copy(source, mate, relay_send.at[source]).start()
    arrive(1)
    for a, b in [(0, 0)] + turns:
        source = alike(a, b, 1 - core)
        coord_copy(source, source, coord_send.at[source]).wait_recv()

    @pl.when(z > 0)
    def _():
        for p in range(cams):
            side_copy(0, p, (y, i), side_send.at[p]).wait_recv()

    @pl.when(z < layers - 1)
    def _():
        for p in range(cams):
            side_copy(1, p, (y, i), side_send.at[p]).wait_recv()

    def expand_block(v, start, width):
        wide = coords[v, :, pl.ds(start - SIDE, width + 2 * SIDE)].astype(f32)
        full = width + 2 * SIDE
        x = jnp.concatenate(
            [
                pltpu.roll(wide, 1, 1)[:, SIDE : SIDE + width],
                wide[:, SIDE : SIDE + width],
                pltpu.roll(wide, full - 1, 1)[:, SIDE : SIDE + width],
            ],
            axis=0,
        ).astype(bf16)
        return jnp.maximum(jnp.dot(first_ref[...], x, preferred_element_type=f32), 0.0)

    def expand_some(begin, end):
        @pl.loop(begin, end)
        def _(n):
            v, s = n // group, n % group
            start = pl.multiple_of(SIDE + s * length, LANES)
            hidden[n] = expand_block(v, start, length).astype(bf16)

    whole = all_cams * group
    expand_some(0, 3 * whole // 4)
    for hop in range(2, layers - 1):
        arrive(hop)
    expand_some(3 * whole // 4, whole)

    slab = lax.broadcasted_iota(jnp.int32, (DEPTH, SIDE), 1)
    low = slab < SIDE // 2
    wide_slab = lax.broadcasted_iota(jnp.int32, (channels, SIDE), 1)
    keep = ((wide_slab < SIDE // 2) & (z < layers - 1)) | ((wide_slab >= SIDE // 2) & (z > 0))
    for v in range(all_cams):
        before = coords[v, :, 0:SIDE].astype(f32)
        begin = coords[v, :, SIDE : 2 * SIDE].astype(f32)
        end = coords[v, :, span : SIDE + span].astype(f32)
        after = coords[v, :, SIDE + span : SIDE + span + SIDE].astype(f32)
        older = jnp.where(slab == 0, pltpu.roll(end, 1, 1), pltpu.roll(after, 1, 1))
        newer = jnp.where(
            slab == SIDE - 1, pltpu.roll(begin, SIDE - 1, 1), pltpu.roll(before, SIDE - 1, 1)
        )
        x = jnp.concatenate(
            [
                jnp.where(low, older, pltpu.roll(before, 1, 1)),
                jnp.where(low, after, before),
                jnp.where(low, pltpu.roll(after, SIDE - 1, 1), newer),
            ],
            axis=0,
        ).astype(bf16)
        h = jnp.maximum(jnp.dot(first_ref[...], x, preferred_element_type=f32), 0.0)
        hidden[whole, :, v * SIDE : (v + 1) * SIDE] = jnp.where(keep, h, 0.0).astype(bf16)

    rates = rates_ref[...]
    decay = jnp.exp(-rates)
    energy = neg_expm1(2.0 * rates)
    drive = jnp.sqrt(energy)

    half = own // 2

    def mix(part):
        stack[...] = jnp.concatenate(
            [weights[o, t] for o in range(4) for t in halves[part]], axis=0
        )
        z_slab = jnp.dot(stack[...], hidden[whole], preferred_element_type=f32)
        for v in range(all_cams):
            piece = z_slab[:, v * SIDE : (v + 1) * SIDE]
            mixed[v, part, :, 0:SIDE] = piece
            mixed[v, part, :, SIDE + span : SIDE + span + SIDE] = piece

        @pl.loop(0, whole)
        def _(n):
            v, s = n // group, n % group
            lanes = pl.ds(pl.multiple_of(SIDE + s * length, LANES), length)
            mixed[v, part, :, lanes] = jnp.dot(
                stack[...], hidden[n], preferred_element_type=f32
            )

    mix(0)
    arrive(layers - 1)
    mix(1)

    def part_copy(slot, source, target, sem):
        return pltpu.make_async_remote_copy(
            src_ref=part_out.at[slot],
            dst_ref=part_in.at[source],
            send_sem=sem,
            recv_sem=part_recv.at[source],
            device_id=(target % cams, z * group + target // cams),
            device_id_type=MESH,
        )

    for d in range(group):
        s = lax.rem(l + d + 1, group)
        centre = pl.ds(pl.multiple_of(SIDE + s * length, LANES), length)
        earlier = pl.ds(pl.multiple_of(s * length, LANES), SIDE + length)
        later = pl.ds(pl.multiple_of(SIDE + s * length, LANES), SIDE + length)
        tops, rests = [], []
        for part in range(2):
            total = jnp.zeros((half, length), f32)
            for v in range(all_cams):
                left = pltpu.roll(mixed[v, part, 0:half, earlier], DILATION_STEP, 1)[:, SIDE:]
                right = pltpu.roll(
                    mixed[v, part, 2 * half : 3 * half, later], SIDE + length - DILATION_STEP, 1
                )[:, :length]
                acc = left + mixed[v, part, half : 2 * half, centre] + right
                kept = mixed[v, part, 3 * half : 4 * half, centre]
                h = (kept + jnp.maximum(acc, 0.0)).astype(bf16)
                mask = coords[v, :, centre].astype(f32)[joints : joints + 1, :]
                total = total + h.astype(f32) * mask
            top = total.astype(bf16)
            tops.append(top)
            rests.append((total - top.astype(f32)).astype(bf16))
        both = jnp.concatenate(tops + rests, axis=0)
        result = jnp.dot(twice, both, preferred_element_type=f32).astype(bf16)
        for p in range(cams):
            part_out[s * cams + p] = result[p * states : (p + 1) * states]
        for p in range(cams):
            target = s * cams + p
            if d < group - 1:
                part_copy(target, me, target, part_send.at[target]).start()
            else:
                @pl.when(p != y)
                def _():
                    part_copy(target, me, target, part_send.at[target]).start()

                @pl.when(p == y)
                def _():
                    part_in[me] = part_out[target]

    seen = jnp.sum(vis_ref[...].astype(f32), axis=0, keepdims=True)
    for d in range(1, members):
        source = lax.rem(me + members - d, members)
        part_copy(source, source, source, part_send.at[source]).wait_recv()
    summed = part_in[0].astype(f32)
    for p in range(1, members):
        summed = summed + part_in[p].astype(f32)
    joined = summed / jnp.maximum(seen, 1.0)

    prod_fwd, (local,) = scan(decay, [drive * joined], False)
    prod_back, (back, through) = scan(decay, [energy * local, energy * prod_fwd], True)

    square = lax.broadcasted_iota(jnp.int32, (states, LANES), 1)
    packed = jnp.where(
        square == 0,
        prod_fwd[:, length - 1 : length],
        jnp.where(
            square == 1,
            local[:, length - 1 : length],
            jnp.where(square == 2, back[:, 0:1], through[:, 0:1]),
        ),
    )
    packed = jnp.concatenate([packed, jnp.zeros((LANES - states, LANES), f32)], axis=0)
    ends[i] = packed.T[0:8]

    def end_copy(source, target, sem):
        return pltpu.make_async_remote_copy(
            src_ref=ends.at[source],
            dst_ref=ends.at[source],
            send_sem=sem,
            recv_sem=end_recv.at[source],
            device_id=(y, target),
            device_id_type=MESH,
        )

    for d in range(1, count):
        target = lax.rem(i + d, count)
        end_copy(i, target, end_send.at[target]).start()
    for d in range(1, count):
        source = lax.rem(i + count - d, count)
        end_copy(source, source, end_send.at[source]).wait_recv()

    entry = jnp.zeros((1, LANES), f32)
    carried = entry
    entries = []
    for j in range(count):
        entries.append(entry)
        carried = jnp.where(j == i, entry, carried)
        entry = ends[j, 0:1] * entry + ends[j, 1:2]
    state = jnp.zeros((1, LANES), f32)
    returned = state
    for j in range(count - 1, -1, -1):
        returned = jnp.where(j == i, state, returned)
        state = ends[j, 0:1] * state + ends[j, 2:3] + ends[j, 3:4] * entries[j]
    both = jnp.concatenate([carried, returned, jnp.zeros((LANES - 2, LANES), f32)], axis=0).T
    out_ref[...] = back + through * both[0:states, 0:1] + prod_back * both[0:states, 1:2]

    for d in range(1, members):
        target = lax.rem(me + d, members)
        part_copy(target, me, target, part_send.at[target]).wait_send()
    coord_copy(me, mate, coord_send.at[mate]).wait_send()
    for a, b in turns:
        target = alike(a, b, core)
        coord_copy(me, target, coord_send.at[target]).wait_send()
        coord_copy(target, mate, relay_send.at[target]).wait_send()
    for d in range(1, count):
        target = lax.rem(i + d, count)
        end_copy(i, target, end_send.at[target]).wait_send()

    @pl.when((l == group - 1) & (z < layers - 1))
    def _():
        for p in range(members):
            side_copy(0, y, (p % cams, (z + 1) * group + p // cams), side_send.at[p]).wait_send()

    @pl.when((l == 0) & (z > 0))
    def _():
        for p in range(members):
            side_copy(1, y, (p % cams, (z - 1) * group + p // cams), side_send.at[p]).wait_send()

    for hop in range(layers - 1):
        @pl.when((z < layers - 1) & (z - hop >= 0))
        def _():
            tap_copy(z - hop, z + 1, up_send, hop == 0).wait_send()

        @pl.when((z > 0) & (z + hop < layers))
        def _():
            tap_copy(z + hop, z - 1, down_send, hop == 0).wait_send()


def block_body(cams, count, group):
    layers = count // group

    def run(keypoints, visibility, expand_weight, dilated_tap_weight, join_weight, decay_rates):
        views, joints, length = keypoints.shape
        channels = expand_weight.shape[2]
        rows = dilated_tap_weight.shape[0] // cams
        own = layers * rows
        members = group * cams
        all_cams = cams * views
        states = decay_rates.shape[0]
        keys = jnp.transpose(keypoints, (1, 0, 2))
        taps = jnp.transpose(dilated_tap_weight, (1, 0, 2))
        extended = group * length + 2 * SIDE
        dma, vmem, bf16 = (pltpu.SemaphoreType.DMA, pltpu.VMEM, jnp.bfloat16)
        return pl.pallas_call(
            functools.partial(block_kernel, cams, layers, group),
            out_shape=jax.ShapeDtypeStruct(decay_rates.shape, jnp.float32),
            in_specs=[pl.BlockSpec(memory_space=pltpu.VMEM)] * 6,
            out_specs=pl.BlockSpec(memory_space=pltpu.VMEM),
            scratch_shapes=[
                vmem((SIDE, channels), jnp.float32),
                vmem((channels, 3 * DEPTH), bf16),
                vmem((all_cams, DEPTH, extended), bf16),
                vmem((all_cams * group + 1, channels, length), bf16),
                vmem((all_cams, 2, 2 * own, extended), jnp.float32),
                vmem((4, layers, rows, channels), bf16),
                vmem((2 * own, channels), bf16),
                vmem((DEPTH, length), jnp.float32),
                vmem((members, states, length), bf16),
                vmem((members, states, length), bf16),
                vmem((count, 8, LANES), jnp.float32),
                dma((members,)),
                dma((members,)),
                dma((members,)),
                dma((members,)),
                dma((2 * cams,)),
                dma((layers,)),
                dma((layers,)),
                dma((layers,)),
                dma((members,)),
                dma((members,)),
                dma((count,)),
                dma((count,)),
            ],
            compiler_params=pltpu.CompilerParams(
                collective_id=0, has_side_effects=True, vmem_limit_bytes=58 * 1024 * 1024
            ),
        )(keys, visibility, expand_weight, taps, join_weight.T, decay_rates)

    return run


def solution(mesh):
    cams, count = mesh.shape["cam"], mesh.shape["tm"]
    group = 4
    fits = count % group == 0 and cams == 2 and count == 4 * group
    return jax.shard_map(
        block_body(cams, count, group) if fits else body,
        mesh=mesh,
        in_specs=(
            P("cam", None, "tm"),
            P(None, "tm"),
            P(),
            P("tm", None, None),
            P(),
            P("cam", "tm"),
        ),
        out_specs=P("cam", "tm"),
        check_vma=False,
    )
```

```python
import functools

import jax
import jax.numpy as jnp
from jax import lax
from jax.experimental import pallas as pl
from jax.experimental.pallas import tpu as pltpu
from jax.sharding import PartitionSpec as P

DILATION_STEP = 3
MESH = pl.DeviceIdType.MESH


def with_halo(array, sides, width):
    for axis, dim in sides:
        count, length = (lax.axis_size(axis), array.shape[dim])
        up = [(i, (i + 1) % count) for i in range(count - 1)]
        down = [(j, i) for i, j in up]
        last = lax.slice_in_dim(array, length - width, length, axis=dim)
        initial = lax.slice_in_dim(array, 0, width, axis=dim)
        before = lax.ppermute(last, axis, up)
        after = lax.ppermute(initial, axis, down)
        array = jnp.concatenate([before, array, after], axis=dim)
    return array


def entering(part, axis, combine, identity, reverse):
    count = lax.axis_size(axis)
    place = lax.axis_index(axis)
    ahead = count - 1 - place if reverse else place
    gathered = jax.tree.map(lambda a: lax.all_gather(a, axis), part)
    state = jax.tree.map(lambda a, e: jnp.zeros_like(a) + jnp.asarray(e, a.dtype), part, identity)

    def one(turn, state):
        source = count - 1 - turn if reverse else turn
        return combine(
            state, jax.tree.map(lambda a: lax.dynamic_index_in_dim(a, source, 0, False), gathered)
        )

    return lax.fori_loop(0, ahead, one, state)


def expand(widened_output, expand_weight, width):
    total = None
    for shift_amount in range(3):
        term = jnp.einsum(
            "vjt,jc->vtc",
            widened_output[:, :, shift_amount : shift_amount + width],
            expand_weight[shift_amount],
            preferred_element_type=jnp.float32,
        )
        total = term if total is None else total + term
    return jax.nn.relu(total).astype(jnp.bfloat16)


def dilate(padded_input, hidden_start0, weight_rows):
    count_of_frames = hidden_start0.shape[1]
    total = None
    for shift_amount in range(3):
        term = jnp.einsum(
            "vti,ni->vtn",
            padded_input[
                :, shift_amount * DILATION_STEP : shift_amount * DILATION_STEP + count_of_frames
            ],
            weight_rows[:, shift_amount],
            preferred_element_type=jnp.float32,
        )
        total = term if total is None else total + term
    residual = hidden_start0.astype(jnp.float32)
    return (residual + jax.nn.relu(total)).astype(jnp.bfloat16)


def chain(earlier, latter):
    return (earlier[0] * latter[0], latter[0] * earlier[1] + latter[1])


def body(keypoints, visibility, expand_weight, dilated_tap_weight, join_weight, decay_rates):
    view_count = keypoints.shape[0]
    count_of_frames = keypoints.shape[2]
    coords = ((keypoints.astype(jnp.float32) - 2048.0) / 2048.0).astype(jnp.bfloat16)
    widened_output = with_halo(coords, (("tm", 2),), 1)
    hidden_start0 = expand(widened_output, expand_weight, count_of_frames)
    padded_input = with_halo(hidden_start0, (("tm", 1),), DILATION_STEP)
    hidden1 = dilate(
        padded_input, hidden_start0, lax.all_gather(dilated_tap_weight, "tm", axis=0, tiled=True)
    )
    own_mask = lax.dynamic_slice_in_dim(
        visibility, lax.axis_index("cam") * view_count, view_count, 0
    )
    masked = hidden1 * own_mask[:, :, None].astype(jnp.bfloat16)
    state_rows = decay_rates.shape[0]
    total = lax.psum_scatter(
        jnp.einsum("vti,is->st", masked, join_weight, preferred_element_type=jnp.float32).astype(
            jnp.bfloat16
        ),
        "cam",
        scatter_dimension=0,
        tiled=True,
    ).astype(jnp.float32)
    seen = jnp.sum(visibility.astype(jnp.float32), axis=0)
    joined = total / jnp.maximum(seen, 1.0)[None, :]
    decay = jnp.exp(-decay_rates)
    energy = -jnp.expm1(-2.0 * decay_rates)
    drive = jnp.sqrt(energy)
    prod_fwd, local_fwd = lax.associative_scan(chain, (decay, drive * joined), axis=1)
    ones_vec = jnp.ones((state_rows,), jnp.float32)
    zeros_vec = jnp.zeros((state_rows,), jnp.float32)
    carried = entering(
        (prod_fwd[:, -1], local_fwd[:, -1]), "tm", chain, (ones_vec, zeros_vec), False
    )
    filtered = local_fwd + prod_fwd * carried[1][:, None]
    prod_back, local_back = lax.associative_scan(
        chain, (decay, energy * filtered), axis=1, reverse=True
    )
    returned = entering(
        (prod_back[:, 0], local_back[:, 0]), "tm", chain, (ones_vec, zeros_vec), True
    )
    smoothed = local_back + prod_back * returned[1][:, None]
    return smoothed

SIDE = 128
DEPTH = 40
LANES = 128


def neg_expm1(u):
    series = jnp.ones_like(u)
    for k in range(11, 1, -1):
        series = 1.0 - series * u * (1.0 / k)
    return jnp.where(u < 0.5, u * series, 1.0 - jnp.exp(-u))


def block_kernel(
    cams, layers, group, keys_ref, vis_ref, raw_ref, taps_ref, join_ref, rates_ref, out_ref,
    first_wide, first_ref, coords, hidden, mixed, weights, stack, powers, kept_forms, stage, part_out, part_in, ends,
    coord_send, coord_recv, relay_send, side_send, side_recv, up_send, down_send, tap_recv,
    part_send, part_recv, end_send, end_recv,
):
    joints, views, length = keys_ref.shape
    channels = raw_ref.shape[2]
    count = layers * group
    all_cams = cams * views
    rows = taps_ref.shape[1] // cams
    own = layers * rows
    states = rates_ref.shape[0]
    members = group * cams
    span = group * length
    f32, bf16 = jnp.float32, jnp.bfloat16
    y = lax.axis_index("cam")
    i = lax.axis_index("tm")
    z = i // group
    l = i % group
    me = l * cams + y

    barrier = pltpu.get_barrier_semaphore()
    turns = [(a, b) for a in range(group // 2) for b in range(cams) if a + b > 0]
    core = l % 2
    mate = (l + 1 - 2 * core) * cams + y

    def alike(a, b, side):
        chip = lax.rem(l // 2 + a, group // 2)
        return (chip * 2 + side) * cams + lax.rem(y + b, cams)

    def greet(cam, tm):
        pl.semaphore_signal(barrier, inc=1, device_id=(cam, tm), device_id_type=MESH)

    greet(y, z * group + mate // cams)
    for a, b in turns:
        target = alike(a, b, core)
        greet(target % cams, z * group + target // cams)

    @pl.when(z > 0)
    def _():
        greet(y, i - group)
        for p in range(cams):
            greet(p, z * group - 1)

    @pl.when(z < layers - 1)
    def _():
        greet(y, i + group)
        for p in range(cams):
            greet(p, (z + 1) * group)

    here = pl.ds(pl.multiple_of(SIDE + l * length, LANES), length)
    for v in range(views):
        stage[...] = jnp.zeros_like(stage)
        stage[pl.ds(0, joints), :] = (keys_ref[:, v, :].astype(f32) - 2048.0) / 2048.0
        stage[pl.ds(joints, 1), :] = vis_ref[pl.ds(y * views + v, 1), :].astype(f32)
        coords[y * views + v, :, here] = stage[...].astype(bf16)

    @pl.when(z == 0)
    def _():
        coords[:, :, 0:SIDE] = jnp.zeros((all_cams, DEPTH, SIDE), bf16)

    @pl.when(z == layers - 1)
    def _():
        coords[:, :, SIDE + span : SIDE + span + SIDE] = jnp.zeros((all_cams, DEPTH, SIDE), bf16)

    first_wide[...] = jnp.zeros_like(first_wide)
    for o in range(3):
        first_wide[pl.ds(o * DEPTH, joints), :] = raw_ref[o].astype(f32)
    first_ref[...] = first_wide[...].T[:, : 3 * DEPTH].astype(bf16)

    for o in range(3):
        weights[o, z] = taps_ref[o, pl.ds(pl.multiple_of(y * rows, rows), rows), :]
    for s in range(layers):
        base = (s * group + l) * (rows * cams) + y * rows
        r = lax.broadcasted_iota(jnp.int32, (rows, channels), 0)
        c = lax.broadcasted_iota(jnp.int32, (rows, channels), 1)
        weights[3, s] = jnp.where(c == r + base, 1.0, 0.0).astype(bf16)
    near = jnp.where(z < layers - 1, z + 1, z - 1)
    far = jnp.where(z == 0, 2, 0)
    last = jnp.where(z < 2, 3, 1)
    halves = ((z, near), (far, last))
    picked = lax.dot_general(
        join_ref[...],
        jnp.concatenate([weights[3, t] for pair in halves for t in pair], axis=0),
        (((1,), (1,)), ((), ())),
        preferred_element_type=f32,
    ).astype(bf16)
    twice = jnp.concatenate([picked, picked], axis=1)

    above = 1 - (z + 1) // layers
    below = (z + layers - 1) // layers
    ends_layer = above * ((l + 1) // group)
    begins_layer = below * (1 - (l + group - 1) // group)
    pl.semaphore_wait(
        barrier, 1 + len(turns) + above + below + members * (ends_layer + begins_layer)
    )

    def tap_copy(source, target, sem, first):
        src = taps_ref.at[:, pl.ds(pl.multiple_of(y * rows, rows), rows), :]
        if not first:
            src = weights.at[pl.ds(0, 3), source]
        return pltpu.make_async_remote_copy(
            src_ref=src,
            dst_ref=weights.at[pl.ds(0, 3), source],
            send_sem=sem.at[source],
            recv_sem=tap_recv.at[source],
            device_id=(y, target * group + l),
            device_id_type=MESH,
        )

    def pass_on(source, upward, first):
        if upward:
            @pl.when(z < layers - 1)
            def _():
                tap_copy(source, z + 1, up_send, first).start()
        else:
            @pl.when(z > 0)
            def _():
                tap_copy(source, z - 1, down_send, first).start()

    def arrive(hop):
        @pl.when(z >= hop)
        def _():
            tap_copy(z - hop, z, up_send, False).wait_recv()
            if hop < layers - 1:
                pass_on(z - hop, True, False)

        @pl.when(z + hop < layers)
        def _():
            tap_copy(z + hop, z, down_send, False).wait_recv()
            if hop < layers - 1:
                pass_on(z + hop, False, False)

    def side_copy(side, sender, target, sem):
        cam_rows = pl.ds(sender * views, views)
        if side == 0:
            src, dst = pl.ds(span, SIDE), pl.ds(0, SIDE)
        else:
            src, dst = pl.ds(SIDE, SIDE), pl.ds(SIDE + span, SIDE)
        return pltpu.make_async_remote_copy(
            src_ref=coords.at[cam_rows, :, src],
            dst_ref=coords.at[cam_rows, :, dst],
            send_sem=sem,
            recv_sem=side_recv.at[side * cams + sender],
            device_id=target,
            device_id_type=MESH,
        )

    def coord_copy(sender, target, sem):
        lanes = pl.ds(pl.multiple_of(SIDE + (sender // cams) * length, LANES), length)
        at = coords.at[pl.ds((sender % cams) * views, views), :, lanes]
        return pltpu.make_async_remote_copy(
            src_ref=at,
            dst_ref=at,
            send_sem=sem,
            recv_sem=coord_recv.at[sender],
            device_id=(target % cams, z * group + target // cams),
            device_id_type=MESH,
        )

    pass_on(z, True, True)
    pass_on(z, False, True)

    coord_copy(me, mate, coord_send.at[mate]).start()
    for a, b in turns:
        target = alike(a, b, core)
        coord_copy(me, target, coord_send.at[target]).start()

    @pl.when((l == group - 1) & (z < layers - 1))
    def _():
        for p in range(members):
            side_copy(0, y, (p % cams, (z + 1) * group + p // cams), side_send.at[p]).start()

    @pl.when((l == 0) & (z > 0))
    def _():
        for p in range(members):
            side_copy(1, y, (p % cams, (z - 1) * group + p // cams), side_send.at[p]).start()

    lane = lax.broadcasted_iota(jnp.int32, (states, length), 1)

    bits = length.bit_length() - 1

    def place(step, reverse):
        turn = length - step if reverse else step
        return turn, (lane < length - step) if reverse else (lane >= step)

    def products(prod, reverse):
        for k in range(bits):
            powers[int(reverse) * bits + k] = prod
            turn, fits = place(1 << k, reverse)
            prod = prod * jnp.where(fits, pltpu.roll(prod, turn, 1), 1.0)
        return prod

    def scan(value, reverse):
        for k in range(bits):
            turn, fits = place(1 << k, reverse)
            moved = jnp.where(fits, pltpu.roll(value, turn, 1), 0.0)
            value = value + powers[int(reverse) * bits + k] * moved
        return value

    rates = rates_ref[...]
    decay = jnp.exp(-rates)
    energy = neg_expm1(2.0 * rates)
    kept_forms[0] = products(decay, False)
    kept_forms[1] = products(decay, True)
    kept_forms[2] = scan(energy * kept_forms[0], True)
    kept_forms[3] = energy
    kept_forms[4] = jnp.sqrt(energy)

    for a, b in turns:
        source = alike(a, b, core)
        coord_copy(source, source, coord_send.at[source]).wait_recv()
        coord_copy(source, mate, relay_send.at[source]).start()
    arrive(1)
    for a, b in [(0, 0)] + turns:
        source = alike(a, b, 1 - core)
        coord_copy(source, source, coord_send.at[source]).wait_recv()

    @pl.when(z > 0)
    def _():
        for p in range(cams):
            side_copy(0, p, (y, i), side_send.at[p]).wait_recv()

    @pl.when(z < layers - 1)
    def _():
        for p in range(cams):
            side_copy(1, p, (y, i), side_send.at[p]).wait_recv()

    def expand_block(v, start, width):
        wide = coords[v, :, pl.ds(start - SIDE, width + 2 * SIDE)].astype(f32)
        full = width + 2 * SIDE
        x = jnp.concatenate(
            [
                pltpu.roll(wide, 1, 1)[:, SIDE : SIDE + width],
                wide[:, SIDE : SIDE + width],
                pltpu.roll(wide, full - 1, 1)[:, SIDE : SIDE + width],
            ],
            axis=0,
        ).astype(bf16)
        return jnp.maximum(jnp.dot(first_ref[...], x, preferred_element_type=f32), 0.0)

    def expand_some(begin, end):
        @pl.loop(begin, end, unroll=2)
        def _(n):
            v, s = n // group, n % group
            start = pl.multiple_of(SIDE + s * length, LANES)
            hidden[n] = expand_block(v, start, length).astype(bf16)

    whole = all_cams * group
    expand_some(0, 3 * whole // 4)
    for hop in range(2, layers - 1):
        arrive(hop)
    expand_some(3 * whole // 4, whole)

    slab = lax.broadcasted_iota(jnp.int32, (DEPTH, SIDE), 1)
    low = slab < SIDE // 2
    wide_slab = lax.broadcasted_iota(jnp.int32, (channels, SIDE), 1)
    keep = ((wide_slab < SIDE // 2) & (z < layers - 1)) | ((wide_slab >= SIDE // 2) & (z > 0))
    for v in range(all_cams):
        before = coords[v, :, 0:SIDE].astype(f32)
        begin = coords[v, :, SIDE : 2 * SIDE].astype(f32)
        end = coords[v, :, span : SIDE + span].astype(f32)
        after = coords[v, :, SIDE + span : SIDE + span + SIDE].astype(f32)
        older = jnp.where(slab == 0, pltpu.roll(end, 1, 1), pltpu.roll(after, 1, 1))
        newer = jnp.where(
            slab == SIDE - 1, pltpu.roll(begin, SIDE - 1, 1), pltpu.roll(before, SIDE - 1, 1)
        )
        x = jnp.concatenate(
            [
                jnp.where(low, older, pltpu.roll(before, 1, 1)),
                jnp.where(low, after, before),
                jnp.where(low, pltpu.roll(after, SIDE - 1, 1), newer),
            ],
            axis=0,
        ).astype(bf16)
        h = jnp.maximum(jnp.dot(first_ref[...], x, preferred_element_type=f32), 0.0)
        hidden[whole, :, v * SIDE : (v + 1) * SIDE] = jnp.where(keep, h, 0.0).astype(bf16)

    arrive(layers - 1)
    for part in range(2):
        stack[pl.ds(part * 2 * own, 2 * own), :] = jnp.concatenate(
            [weights[o, t] for o in range(4) for t in halves[part]], axis=0
        )
    z_slab = jnp.dot(stack[...], hidden[whole], preferred_element_type=f32)
    z_slab = z_slab.reshape(2, 2 * own, length)
    for v in range(all_cams):
        piece = z_slab[:, :, v * SIDE : (v + 1) * SIDE]
        mixed[v, :, :, 0:SIDE] = piece
        mixed[v, :, :, SIDE + span : SIDE + span + SIDE] = piece

    @pl.loop(0, whole, unroll=4)
    def _(n):
        v, s = n // group, n % group
        lanes = pl.ds(pl.multiple_of(SIDE + s * length, LANES), length)
        mixed[v, :, :, lanes] = jnp.dot(
            stack[...], hidden[n], preferred_element_type=f32
        ).reshape(2, 2 * own, length)

    half = own // 2

    def part_copy(slot, source, target, sem):
        return pltpu.make_async_remote_copy(
            src_ref=part_out.at[slot],
            dst_ref=part_in.at[source],
            send_sem=sem,
            recv_sem=part_recv.at[source],
            device_id=(target % cams, z * group + target // cams),
            device_id_type=MESH,
        )

    for d in range(group):
        s = lax.rem(l + d + 1, group)
        centre = pl.ds(pl.multiple_of(SIDE + s * length, LANES), length)
        earlier = pl.ds(pl.multiple_of(s * length, LANES), SIDE + length)
        later = pl.ds(pl.multiple_of(SIDE + s * length, LANES), SIDE + length)
        tops, rests = [], []
        for part in range(2):
            total = jnp.zeros((half, length), f32)
            for v in range(all_cams):
                left = pltpu.roll(mixed[v, part, 0:half, earlier], DILATION_STEP, 1)[:, SIDE:]
                right = pltpu.roll(
                    mixed[v, part, 2 * half : 3 * half, later], SIDE + length - DILATION_STEP, 1
                )[:, :length]
                acc = left + mixed[v, part, half : 2 * half, centre] + right
                kept = mixed[v, part, 3 * half : 4 * half, centre]
                h = (kept + jnp.maximum(acc, 0.0)).astype(bf16)
                mask = coords[v, :, centre].astype(f32)[joints : joints + 1, :]
                total = total + h.astype(f32) * mask
            top = total.astype(bf16)
            tops.append(top)
            rests.append((total - top.astype(f32)).astype(bf16))
        both = jnp.concatenate(tops + rests, axis=0)
        result = jnp.dot(twice, both, preferred_element_type=f32).astype(bf16)
        for p in range(cams):
            part_out[s * cams + p] = result[p * states : (p + 1) * states]
        for p in range(cams):
            target = s * cams + p
            if d < group - 1:
                part_copy(target, me, target, part_send.at[target]).start()
            else:
                @pl.when(p != y)
                def _():
                    part_copy(target, me, target, part_send.at[target]).start()

                @pl.when(p == y)
                def _():
                    part_in[me] = part_out[target]

    seen = jnp.sum(vis_ref[...].astype(f32), axis=0, keepdims=True)
    for d in range(1, members):
        source = lax.rem(me + members - d, members)
        part_copy(source, source, source, part_send.at[source]).wait_recv()
    summed = part_in[0].astype(f32)
    for p in range(1, members):
        summed = summed + part_in[p].astype(f32)
    joined = summed / jnp.maximum(seen, 1.0)

    local = scan(kept_forms[4] * joined, False)
    back = scan(kept_forms[3] * local, True)
    prod_fwd, prod_back, through = kept_forms[0], kept_forms[1], kept_forms[2]

    square = lax.broadcasted_iota(jnp.int32, (states, LANES), 1)
    packed = jnp.where(
        square == 0,
        prod_fwd[:, length - 1 : length],
        jnp.where(
            square == 1,
            local[:, length - 1 : length],
            jnp.where(square == 2, back[:, 0:1], through[:, 0:1]),
        ),
    )
    packed = jnp.concatenate([packed, jnp.zeros((LANES - states, LANES), f32)], axis=0)
    ends[i] = packed.T[0:8]

    def end_copy(source, target, sem):
        return pltpu.make_async_remote_copy(
            src_ref=ends.at[source],
            dst_ref=ends.at[source],
            send_sem=sem,
            recv_sem=end_recv.at[source],
            device_id=(y, target),
            device_id_type=MESH,
        )

    for d in range(1, count):
        target = lax.rem(i + d, count)
        end_copy(i, target, end_send.at[target]).start()
    for d in range(1, count):
        source = lax.rem(i + count - d, count)
        end_copy(source, source, end_send.at[source]).wait_recv()

    entry = jnp.zeros((1, LANES), f32)
    carried = entry
    entries = []
    for j in range(count):
        entries.append(entry)
        carried = jnp.where(j == i, entry, carried)
        entry = ends[j, 0:1] * entry + ends[j, 1:2]
    state = jnp.zeros((1, LANES), f32)
    returned = state
    for j in range(count - 1, -1, -1):
        returned = jnp.where(j == i, state, returned)
        state = ends[j, 0:1] * state + ends[j, 2:3] + ends[j, 3:4] * entries[j]
    both = jnp.concatenate([carried, returned, jnp.zeros((LANES - 2, LANES), f32)], axis=0).T
    out_ref[...] = back + through * both[0:states, 0:1] + prod_back * both[0:states, 1:2]

    for d in range(1, members):
        target = lax.rem(me + d, members)
        part_copy(target, me, target, part_send.at[target]).wait_send()
    coord_copy(me, mate, coord_send.at[mate]).wait_send()
    for a, b in turns:
        target = alike(a, b, core)
        coord_copy(me, target, coord_send.at[target]).wait_send()
        coord_copy(target, mate, relay_send.at[target]).wait_send()
    for d in range(1, count):
        target = lax.rem(i + d, count)
        end_copy(i, target, end_send.at[target]).wait_send()

    @pl.when((l == group - 1) & (z < layers - 1))
    def _():
        for p in range(members):
            side_copy(0, y, (p % cams, (z + 1) * group + p // cams), side_send.at[p]).wait_send()

    @pl.when((l == 0) & (z > 0))
    def _():
        for p in range(members):
            side_copy(1, y, (p % cams, (z - 1) * group + p // cams), side_send.at[p]).wait_send()

    for hop in range(layers - 1):
        @pl.when((z < layers - 1) & (z - hop >= 0))
        def _():
            tap_copy(z - hop, z + 1, up_send, hop == 0).wait_send()

        @pl.when((z > 0) & (z + hop < layers))
        def _():
            tap_copy(z + hop, z - 1, down_send, hop == 0).wait_send()


def block_body(cams, count, group):
    layers = count // group

    def run(keypoints, visibility, expand_weight, dilated_tap_weight, join_weight, decay_rates):
        views, joints, length = keypoints.shape
        channels = expand_weight.shape[2]
        rows = dilated_tap_weight.shape[0] // cams
        own = layers * rows
        members = group * cams
        all_cams = cams * views
        states = decay_rates.shape[0]
        keys = jnp.transpose(keypoints, (1, 0, 2))
        taps = jnp.transpose(dilated_tap_weight, (1, 0, 2))
        extended = group * length + 2 * SIDE
        dma, vmem, bf16 = (pltpu.SemaphoreType.DMA, pltpu.VMEM, jnp.bfloat16)
        return pl.pallas_call(
            functools.partial(block_kernel, cams, layers, group),
            out_shape=jax.ShapeDtypeStruct(decay_rates.shape, jnp.float32),
            in_specs=[pl.BlockSpec(memory_space=pltpu.VMEM)] * 6,
            out_specs=pl.BlockSpec(memory_space=pltpu.VMEM),
            scratch_shapes=[
                vmem((SIDE, channels), jnp.float32),
                vmem((channels, 3 * DEPTH), bf16),
                vmem((all_cams, DEPTH, extended), bf16),
                vmem((all_cams * group + 1, channels, length), bf16),
                vmem((all_cams, 2, 2 * own, extended), jnp.float32),
                vmem((4, layers, rows, channels), bf16),
                vmem((4 * own, channels), bf16),
                vmem((2 * (length.bit_length() - 1), states, length), jnp.float32),
                vmem((5, states, length), jnp.float32),
                vmem((DEPTH, length), jnp.float32),
                vmem((members, states, length), bf16),
                vmem((members, states, length), bf16),
                vmem((count, 8, LANES), jnp.float32),
                dma((members,)),
                dma((members,)),
                dma((members,)),
                dma((members,)),
                dma((2 * cams,)),
                dma((layers,)),
                dma((layers,)),
                dma((layers,)),
                dma((members,)),
                dma((members,)),
                dma((count,)),
                dma((count,)),
            ],
            compiler_params=pltpu.CompilerParams(
                collective_id=0, has_side_effects=True, vmem_limit_bytes=58 * 1024 * 1024
            ),
        )(keys, visibility, expand_weight, taps, join_weight.T, decay_rates)

    return run


def solution(mesh):
    cams, count = mesh.shape["cam"], mesh.shape["tm"]
    group = 4
    fits = count % group == 0 and cams == 2 and count == 4 * group
    return jax.shard_map(
        block_body(cams, count, group) if fits else body,
        mesh=mesh,
        in_specs=(
            P("cam", None, "tm"),
            P(None, "tm"),
            P(),
            P("tm", None, None),
            P(),
            P("cam", "tm"),
        ),
        out_specs=P("cam", "tm"),
        check_vma=False,
    )
```

```python
import functools

import jax
import jax.numpy as jnp
from jax import lax
from jax.experimental import pallas as pl
from jax.experimental.pallas import tpu as pltpu
from jax.sharding import PartitionSpec as P

DILATION_STEP = 3
MESH = pl.DeviceIdType.MESH


def with_halo(array, sides, width):
    for axis, dim in sides:
        count, length = (lax.axis_size(axis), array.shape[dim])
        up = [(i, (i + 1) % count) for i in range(count - 1)]
        down = [(j, i) for i, j in up]
        last = lax.slice_in_dim(array, length - width, length, axis=dim)
        initial = lax.slice_in_dim(array, 0, width, axis=dim)
        before = lax.ppermute(last, axis, up)
        after = lax.ppermute(initial, axis, down)
        array = jnp.concatenate([before, array, after], axis=dim)
    return array


def entering(part, axis, combine, identity, reverse):
    count = lax.axis_size(axis)
    place = lax.axis_index(axis)
    ahead = count - 1 - place if reverse else place
    gathered = jax.tree.map(lambda a: lax.all_gather(a, axis), part)
    state = jax.tree.map(lambda a, e: jnp.zeros_like(a) + jnp.asarray(e, a.dtype), part, identity)

    def one(turn, state):
        source = count - 1 - turn if reverse else turn
        return combine(
            state, jax.tree.map(lambda a: lax.dynamic_index_in_dim(a, source, 0, False), gathered)
        )

    return lax.fori_loop(0, ahead, one, state)


def expand(widened_output, expand_weight, width):
    total = None
    for shift_amount in range(3):
        term = jnp.einsum(
            "vjt,jc->vtc",
            widened_output[:, :, shift_amount : shift_amount + width],
            expand_weight[shift_amount],
            preferred_element_type=jnp.float32,
        )
        total = term if total is None else total + term
    return jax.nn.relu(total).astype(jnp.bfloat16)


def dilate(padded_input, hidden_start0, weight_rows):
    count_of_frames = hidden_start0.shape[1]
    total = None
    for shift_amount in range(3):
        term = jnp.einsum(
            "vti,ni->vtn",
            padded_input[
                :, shift_amount * DILATION_STEP : shift_amount * DILATION_STEP + count_of_frames
            ],
            weight_rows[:, shift_amount],
            preferred_element_type=jnp.float32,
        )
        total = term if total is None else total + term
    residual = hidden_start0.astype(jnp.float32)
    return (residual + jax.nn.relu(total)).astype(jnp.bfloat16)


def chain(earlier, latter):
    return (earlier[0] * latter[0], latter[0] * earlier[1] + latter[1])


def body(keypoints, visibility, expand_weight, dilated_tap_weight, join_weight, decay_rates):
    view_count = keypoints.shape[0]
    count_of_frames = keypoints.shape[2]
    coords = ((keypoints.astype(jnp.float32) - 2048.0) / 2048.0).astype(jnp.bfloat16)
    widened_output = with_halo(coords, (("tm", 2),), 1)
    hidden_start0 = expand(widened_output, expand_weight, count_of_frames)
    padded_input = with_halo(hidden_start0, (("tm", 1),), DILATION_STEP)
    hidden1 = dilate(
        padded_input, hidden_start0, lax.all_gather(dilated_tap_weight, "tm", axis=0, tiled=True)
    )
    own_mask = lax.dynamic_slice_in_dim(
        visibility, lax.axis_index("cam") * view_count, view_count, 0
    )
    masked = hidden1 * own_mask[:, :, None].astype(jnp.bfloat16)
    state_rows = decay_rates.shape[0]
    total = lax.psum_scatter(
        jnp.einsum("vti,is->st", masked, join_weight, preferred_element_type=jnp.float32).astype(
            jnp.bfloat16
        ),
        "cam",
        scatter_dimension=0,
        tiled=True,
    ).astype(jnp.float32)
    seen = jnp.sum(visibility.astype(jnp.float32), axis=0)
    joined = total / jnp.maximum(seen, 1.0)[None, :]
    decay = jnp.exp(-decay_rates)
    energy = -jnp.expm1(-2.0 * decay_rates)
    drive = jnp.sqrt(energy)
    prod_fwd, local_fwd = lax.associative_scan(chain, (decay, drive * joined), axis=1)
    ones_vec = jnp.ones((state_rows,), jnp.float32)
    zeros_vec = jnp.zeros((state_rows,), jnp.float32)
    carried = entering(
        (prod_fwd[:, -1], local_fwd[:, -1]), "tm", chain, (ones_vec, zeros_vec), False
    )
    filtered = local_fwd + prod_fwd * carried[1][:, None]
    prod_back, local_back = lax.associative_scan(
        chain, (decay, energy * filtered), axis=1, reverse=True
    )
    returned = entering(
        (prod_back[:, 0], local_back[:, 0]), "tm", chain, (ones_vec, zeros_vec), True
    )
    smoothed = local_back + prod_back * returned[1][:, None]
    return smoothed

SIDE = 128
DEPTH = 40
LANES = 128


def neg_expm1(u):
    series = jnp.ones_like(u)
    for k in range(11, 1, -1):
        series = 1.0 - series * u * (1.0 / k)
    return jnp.where(u < 0.5, u * series, 1.0 - jnp.exp(-u))


def block_kernel(
    cams, layers, group, keys_ref, vis_ref, raw_ref, taps_ref, join_ref, rates_ref, out_ref,
    first_wide, first_ref, coords, hidden, mixed, weights, stack, powers, kept_forms, stage, part_out, part_in, ends,
    coord_send, coord_recv, relay_send, side_send, side_recv, up_send, down_send, tap_recv,
    part_send, part_recv, end_send, end_recv,
):
    joints, views, length = keys_ref.shape
    channels = raw_ref.shape[2]
    count = layers * group
    all_cams = cams * views
    rows = taps_ref.shape[1] // cams
    own = layers * rows
    states = rates_ref.shape[0]
    members = group * cams
    span = group * length
    f32, bf16 = jnp.float32, jnp.bfloat16
    y = lax.axis_index("cam")
    i = lax.axis_index("tm")
    z = i // group
    l = i % group
    me = l * cams + y

    barrier = pltpu.get_barrier_semaphore()
    turns = [(a, b) for a in range(group // 2) for b in range(cams) if a + b > 0]
    core = l % 2
    mate = (l + 1 - 2 * core) * cams + y

    def alike(a, b, side):
        chip = lax.rem(l // 2 + a, group // 2)
        return (chip * 2 + side) * cams + lax.rem(y + b, cams)

    def greet(cam, tm):
        pl.semaphore_signal(barrier, inc=1, device_id=(cam, tm), device_id_type=MESH)

    greet(y, z * group + mate // cams)
    for a, b in turns:
        target = alike(a, b, core)
        greet(target % cams, z * group + target // cams)

    @pl.when(z > 0)
    def _():
        greet(y, i - group)
        for p in range(cams):
            greet(p, z * group - 1)

    @pl.when(z < layers - 1)
    def _():
        greet(y, i + group)
        for p in range(cams):
            greet(p, (z + 1) * group)

    here = pl.ds(pl.multiple_of(SIDE + l * length, LANES), length)
    for v in range(views):
        stage[...] = jnp.zeros_like(stage)
        stage[pl.ds(0, joints), :] = (keys_ref[:, v, :].astype(f32) - 2048.0) / 2048.0
        stage[pl.ds(joints, 1), :] = vis_ref[pl.ds(y * views + v, 1), :].astype(f32)
        coords[y * views + v, :, here] = stage[...].astype(bf16)

    @pl.when(z == 0)
    def _():
        coords[:, :, 0:SIDE] = jnp.zeros((all_cams, DEPTH, SIDE), bf16)

    @pl.when(z == layers - 1)
    def _():
        coords[:, :, SIDE + span : SIDE + span + SIDE] = jnp.zeros((all_cams, DEPTH, SIDE), bf16)

    first_wide[...] = jnp.zeros_like(first_wide)
    for o in range(3):
        first_wide[pl.ds(o * DEPTH, joints), :] = raw_ref[o].astype(f32)
    first_ref[...] = first_wide[...].T[:, : 3 * DEPTH].astype(bf16)

    for o in range(3):
        weights[o, z] = taps_ref[o, pl.ds(pl.multiple_of(y * rows, rows), rows), :]
    for s in range(layers):
        base = (s * group + l) * (rows * cams) + y * rows
        r = lax.broadcasted_iota(jnp.int32, (rows, channels), 0)
        c = lax.broadcasted_iota(jnp.int32, (rows, channels), 1)
        weights[3, s] = jnp.where(c == r + base, 1.0, 0.0).astype(bf16)
    near = jnp.where(z < layers - 1, z + 1, z - 1)
    far = jnp.where(z == 0, 2, 0)
    last = jnp.where(z < 2, 3, 1)
    halves = ((z, near), (far, last))
    picked = lax.dot_general(
        join_ref[...],
        jnp.concatenate([weights[3, t] for pair in halves for t in pair], axis=0),
        (((1,), (1,)), ((), ())),
        preferred_element_type=f32,
    ).astype(bf16)
    twice = jnp.concatenate([picked, picked], axis=1)

    above = 1 - (z + 1) // layers
    below = (z + layers - 1) // layers
    ends_layer = above * ((l + 1) // group)
    begins_layer = below * (1 - (l + group - 1) // group)
    pl.semaphore_wait(
        barrier, 1 + len(turns) + above + below + members * (ends_layer + begins_layer)
    )

    def tap_copy(source, target, sem, first):
        src = taps_ref.at[:, pl.ds(pl.multiple_of(y * rows, rows), rows), :]
        if not first:
            src = weights.at[pl.ds(0, 3), source]
        return pltpu.make_async_remote_copy(
            src_ref=src,
            dst_ref=weights.at[pl.ds(0, 3), source],
            send_sem=sem.at[source],
            recv_sem=tap_recv.at[source],
            device_id=(y, target * group + l),
            device_id_type=MESH,
        )

    def pass_on(source, upward, first):
        if upward:
            @pl.when(z < layers - 1)
            def _():
                tap_copy(source, z + 1, up_send, first).start()
        else:
            @pl.when(z > 0)
            def _():
                tap_copy(source, z - 1, down_send, first).start()

    def arrive(hop):
        @pl.when(z >= hop)
        def _():
            tap_copy(z - hop, z, up_send, False).wait_recv()
            if hop < layers - 1:
                pass_on(z - hop, True, False)

        @pl.when(z + hop < layers)
        def _():
            tap_copy(z + hop, z, down_send, False).wait_recv()
            if hop < layers - 1:
                pass_on(z + hop, False, False)

    def side_copy(side, sender, target, sem):
        cam_rows = pl.ds(sender * views, views)
        if side == 0:
            src, dst = pl.ds(span, SIDE), pl.ds(0, SIDE)
        else:
            src, dst = pl.ds(SIDE, SIDE), pl.ds(SIDE + span, SIDE)
        return pltpu.make_async_remote_copy(
            src_ref=coords.at[cam_rows, :, src],
            dst_ref=coords.at[cam_rows, :, dst],
            send_sem=sem,
            recv_sem=side_recv.at[side * cams + sender],
            device_id=target,
            device_id_type=MESH,
        )

    def coord_copy(sender, target, sem):
        lanes = pl.ds(pl.multiple_of(SIDE + (sender // cams) * length, LANES), length)
        at = coords.at[pl.ds((sender % cams) * views, views), :, lanes]
        return pltpu.make_async_remote_copy(
            src_ref=at,
            dst_ref=at,
            send_sem=sem,
            recv_sem=coord_recv.at[sender],
            device_id=(target % cams, z * group + target // cams),
            device_id_type=MESH,
        )

    pass_on(z, True, True)
    pass_on(z, False, True)

    coord_copy(me, mate, coord_send.at[mate]).start()
    for a, b in turns:
        target = alike(a, b, core)
        coord_copy(me, target, coord_send.at[target]).start()

    @pl.when((l == group - 1) & (z < layers - 1))
    def _():
        for p in range(members):
            side_copy(0, y, (p % cams, (z + 1) * group + p // cams), side_send.at[p]).start()

    @pl.when((l == 0) & (z > 0))
    def _():
        for p in range(members):
            side_copy(1, y, (p % cams, (z - 1) * group + p // cams), side_send.at[p]).start()

    lane = lax.broadcasted_iota(jnp.int32, (states, length), 1)

    bits = length.bit_length() - 1

    def place(step, reverse):
        turn = length - step if reverse else step
        return turn, (lane < length - step) if reverse else (lane >= step)

    def products(prod, reverse):
        for k in range(bits):
            powers[int(reverse) * bits + k] = prod
            turn, fits = place(1 << k, reverse)
            prod = prod * jnp.where(fits, pltpu.roll(prod, turn, 1), 1.0)
        return prod

    def scan(value, reverse):
        for k in range(bits):
            turn, fits = place(1 << k, reverse)
            moved = jnp.where(fits, pltpu.roll(value, turn, 1), 0.0)
            value = value + powers[int(reverse) * bits + k] * moved
        return value

    rates = rates_ref[...]
    decay = jnp.exp(-rates)
    energy = neg_expm1(2.0 * rates)
    kept_forms[0] = products(decay, False)
    kept_forms[1] = products(decay, True)
    kept_forms[2] = scan(energy * kept_forms[0], True)
    kept_forms[3] = energy
    kept_forms[4] = jnp.sqrt(energy)

    for a, b in turns:
        source = alike(a, b, core)
        coord_copy(source, source, coord_send.at[source]).wait_recv()
        coord_copy(source, mate, relay_send.at[source]).start()
    arrive(1)
    for a, b in [(0, 0)] + turns:
        source = alike(a, b, 1 - core)
        coord_copy(source, source, coord_send.at[source]).wait_recv()

    @pl.when(z > 0)
    def _():
        for p in range(cams):
            side_copy(0, p, (y, i), side_send.at[p]).wait_recv()

    @pl.when(z < layers - 1)
    def _():
        for p in range(cams):
            side_copy(1, p, (y, i), side_send.at[p]).wait_recv()

    def expand_block(v, start, width):
        wide = coords[v, :, pl.ds(start - SIDE, width + 2 * SIDE)].astype(f32)
        full = width + 2 * SIDE
        x = jnp.concatenate(
            [
                pltpu.roll(wide, 1, 1)[:, SIDE : SIDE + width],
                wide[:, SIDE : SIDE + width],
                pltpu.roll(wide, full - 1, 1)[:, SIDE : SIDE + width],
            ],
            axis=0,
        ).astype(bf16)
        return jnp.maximum(jnp.dot(first_ref[...], x, preferred_element_type=f32), 0.0)

    def expand_some(begin, end):
        @pl.loop(begin, end, unroll=2)
        def _(n):
            v, s = n // group, n % group
            start = pl.multiple_of(SIDE + s * length, LANES)
            hidden[n] = expand_block(v, start, length).astype(bf16)

    whole = all_cams * group
    expand_some(0, whole // 4)
    for hop in range(2, layers - 1):
        arrive(hop)
    expand_some(whole // 4, whole)

    slab = lax.broadcasted_iota(jnp.int32, (DEPTH, SIDE), 1)
    low = slab < SIDE // 2
    wide_slab = lax.broadcasted_iota(jnp.int32, (channels, SIDE), 1)
    keep = ((wide_slab < SIDE // 2) & (z < layers - 1)) | ((wide_slab >= SIDE // 2) & (z > 0))
    for v in range(all_cams):
        before = coords[v, :, 0:SIDE].astype(f32)
        begin = coords[v, :, SIDE : 2 * SIDE].astype(f32)
        end = coords[v, :, span : SIDE + span].astype(f32)
        after = coords[v, :, SIDE + span : SIDE + span + SIDE].astype(f32)
        older = jnp.where(slab == 0, pltpu.roll(end, 1, 1), pltpu.roll(after, 1, 1))
        newer = jnp.where(
            slab == SIDE - 1, pltpu.roll(begin, SIDE - 1, 1), pltpu.roll(before, SIDE - 1, 1)
        )
        x = jnp.concatenate(
            [
                jnp.where(low, older, pltpu.roll(before, 1, 1)),
                jnp.where(low, after, before),
                jnp.where(low, pltpu.roll(after, SIDE - 1, 1), newer),
            ],
            axis=0,
        ).astype(bf16)
        h = jnp.maximum(jnp.dot(first_ref[...], x, preferred_element_type=f32), 0.0)
        hidden[whole, :, v * SIDE : (v + 1) * SIDE] = jnp.where(keep, h, 0.0).astype(bf16)

    arrive(layers - 1)
    for part in range(2):
        stack[pl.ds(part * 2 * own, 2 * own), :] = jnp.concatenate(
            [weights[o, t] for o in range(4) for t in halves[part]], axis=0
        )
    z_slab = jnp.dot(stack[...], hidden[whole], preferred_element_type=f32)
    z_slab = z_slab.reshape(2, 2 * own, length)
    for v in range(all_cams):
        piece = z_slab[:, :, v * SIDE : (v + 1) * SIDE]
        mixed[v, :, :, 0:SIDE] = piece
        mixed[v, :, :, SIDE + span : SIDE + span + SIDE] = piece

    @pl.loop(0, whole, unroll=4)
    def _(n):
        v, s = n // group, n % group
        lanes = pl.ds(pl.multiple_of(SIDE + s * length, LANES), length)
        mixed[v, :, :, lanes] = jnp.dot(
            stack[...], hidden[n], preferred_element_type=f32
        ).reshape(2, 2 * own, length)

    half = own // 2

    def part_copy(slot, source, target, sem):
        return pltpu.make_async_remote_copy(
            src_ref=part_out.at[slot],
            dst_ref=part_in.at[source],
            send_sem=sem,
            recv_sem=part_recv.at[source],
            device_id=(target % cams, z * group + target // cams),
            device_id_type=MESH,
        )

    for d in range(group):
        s = lax.rem(l + d + 1, group)
        centre = pl.ds(pl.multiple_of(SIDE + s * length, LANES), length)
        earlier = pl.ds(pl.multiple_of(s * length, LANES), SIDE + length)
        later = pl.ds(pl.multiple_of(SIDE + s * length, LANES), SIDE + length)
        tops, rests = [], []
        for part in range(2):
            total = jnp.zeros((half, length), f32)
            for v in range(all_cams):
                left = pltpu.roll(mixed[v, part, 0:half, earlier], DILATION_STEP, 1)[:, SIDE:]
                right = pltpu.roll(
                    mixed[v, part, 2 * half : 3 * half, later], SIDE + length - DILATION_STEP, 1
                )[:, :length]
                acc = left + mixed[v, part, half : 2 * half, centre] + right
                kept = mixed[v, part, 3 * half : 4 * half, centre]
                h = (kept + jnp.maximum(acc, 0.0)).astype(bf16)
                mask = coords[v, :, centre].astype(f32)[joints : joints + 1, :]
                total = total + h.astype(f32) * mask
            top = total.astype(bf16)
            tops.append(top)
            rests.append((total - top.astype(f32)).astype(bf16))
        both = jnp.concatenate(tops + rests, axis=0)
        result = jnp.dot(twice, both, preferred_element_type=f32).astype(bf16)
        for p in range(cams):
            part_out[s * cams + p] = result[p * states : (p + 1) * states]
        for p in range(cams):
            target = s * cams + p
            if d < group - 1:
                part_copy(target, me, target, part_send.at[target]).start()
            else:
                @pl.when(p != y)
                def _():
                    part_copy(target, me, target, part_send.at[target]).start()

                @pl.when(p == y)
                def _():
                    part_in[me] = part_out[target]

    seen = jnp.sum(vis_ref[...].astype(f32), axis=0, keepdims=True)
    for d in range(1, members):
        source = lax.rem(me + members - d, members)
        part_copy(source, source, source, part_send.at[source]).wait_recv()
    summed = part_in[0].astype(f32)
    for p in range(1, members):
        summed = summed + part_in[p].astype(f32)
    joined = summed / jnp.maximum(seen, 1.0)

    local = scan(kept_forms[4] * joined, False)
    back = scan(kept_forms[3] * local, True)
    prod_fwd, prod_back, through = kept_forms[0], kept_forms[1], kept_forms[2]

    square = lax.broadcasted_iota(jnp.int32, (states, LANES), 1)
    packed = jnp.where(
        square == 0,
        prod_fwd[:, length - 1 : length],
        jnp.where(
            square == 1,
            local[:, length - 1 : length],
            jnp.where(square == 2, back[:, 0:1], through[:, 0:1]),
        ),
    )
    packed = jnp.concatenate([packed, jnp.zeros((LANES - states, LANES), f32)], axis=0)
    ends[i] = packed.T[0:8]

    def end_copy(source, target, sem):
        return pltpu.make_async_remote_copy(
            src_ref=ends.at[source],
            dst_ref=ends.at[source],
            send_sem=sem,
            recv_sem=end_recv.at[source],
            device_id=(y, target),
            device_id_type=MESH,
        )

    for d in range(1, count):
        target = lax.rem(i + d, count)
        end_copy(i, target, end_send.at[target]).start()
    for d in range(1, count):
        source = lax.rem(i + count - d, count)
        end_copy(source, source, end_send.at[source]).wait_recv()

    entry = jnp.zeros((1, LANES), f32)
    carried = entry
    entries = []
    for j in range(count):
        entries.append(entry)
        carried = jnp.where(j == i, entry, carried)
        entry = ends[j, 0:1] * entry + ends[j, 1:2]
    state = jnp.zeros((1, LANES), f32)
    returned = state
    for j in range(count - 1, -1, -1):
        returned = jnp.where(j == i, state, returned)
        state = ends[j, 0:1] * state + ends[j, 2:3] + ends[j, 3:4] * entries[j]
    both = jnp.concatenate([carried, returned, jnp.zeros((LANES - 2, LANES), f32)], axis=0).T
    out_ref[...] = back + through * both[0:states, 0:1] + prod_back * both[0:states, 1:2]

    for d in range(1, members):
        target = lax.rem(me + d, members)
        part_copy(target, me, target, part_send.at[target]).wait_send()
    coord_copy(me, mate, coord_send.at[mate]).wait_send()
    for a, b in turns:
        target = alike(a, b, core)
        coord_copy(me, target, coord_send.at[target]).wait_send()
        coord_copy(target, mate, relay_send.at[target]).wait_send()
    for d in range(1, count):
        target = lax.rem(i + d, count)
        end_copy(i, target, end_send.at[target]).wait_send()

    @pl.when((l == group - 1) & (z < layers - 1))
    def _():
        for p in range(members):
            side_copy(0, y, (p % cams, (z + 1) * group + p // cams), side_send.at[p]).wait_send()

    @pl.when((l == 0) & (z > 0))
    def _():
        for p in range(members):
            side_copy(1, y, (p % cams, (z - 1) * group + p // cams), side_send.at[p]).wait_send()

    for hop in range(layers - 1):
        @pl.when((z < layers - 1) & (z - hop >= 0))
        def _():
            tap_copy(z - hop, z + 1, up_send, hop == 0).wait_send()

        @pl.when((z > 0) & (z + hop < layers))
        def _():
            tap_copy(z + hop, z - 1, down_send, hop == 0).wait_send()


def block_body(cams, count, group):
    layers = count // group

    def run(keypoints, visibility, expand_weight, dilated_tap_weight, join_weight, decay_rates):
        views, joints, length = keypoints.shape
        channels = expand_weight.shape[2]
        rows = dilated_tap_weight.shape[0] // cams
        own = layers * rows
        members = group * cams
        all_cams = cams * views
        states = decay_rates.shape[0]
        keys = jnp.transpose(keypoints, (1, 0, 2))
        taps = jnp.transpose(dilated_tap_weight, (1, 0, 2))
        extended = group * length + 2 * SIDE
        dma, vmem, bf16 = (pltpu.SemaphoreType.DMA, pltpu.VMEM, jnp.bfloat16)
        return pl.pallas_call(
            functools.partial(block_kernel, cams, layers, group),
            out_shape=jax.ShapeDtypeStruct(decay_rates.shape, jnp.float32),
            in_specs=[pl.BlockSpec(memory_space=pltpu.VMEM)] * 6,
            out_specs=pl.BlockSpec(memory_space=pltpu.VMEM),
            scratch_shapes=[
                vmem((SIDE, channels), jnp.float32),
                vmem((channels, 3 * DEPTH), bf16),
                vmem((all_cams, DEPTH, extended), bf16),
                vmem((all_cams * group + 1, channels, length), bf16),
                vmem((all_cams, 2, 2 * own, extended), jnp.float32),
                vmem((4, layers, rows, channels), bf16),
                vmem((4 * own, channels), bf16),
                vmem((2 * (length.bit_length() - 1), states, length), jnp.float32),
                vmem((5, states, length), jnp.float32),
                vmem((DEPTH, length), jnp.float32),
                vmem((members, states, length), bf16),
                vmem((members, states, length), bf16),
                vmem((count, 8, LANES), jnp.float32),
                dma((members,)),
                dma((members,)),
                dma((members,)),
                dma((members,)),
                dma((2 * cams,)),
                dma((layers,)),
                dma((layers,)),
                dma((layers,)),
                dma((members,)),
                dma((members,)),
                dma((count,)),
                dma((count,)),
            ],
            compiler_params=pltpu.CompilerParams(
                collective_id=0, has_side_effects=True, vmem_limit_bytes=58 * 1024 * 1024
            ),
        )(keys, visibility, expand_weight, taps, join_weight.T, decay_rates)

    return run


def solution(mesh):
    cams, count = mesh.shape["cam"], mesh.shape["tm"]
    group = 4
    fits = count % group == 0 and cams == 2 and count == 4 * group
    return jax.shard_map(
        block_body(cams, count, group) if fits else body,
        mesh=mesh,
        in_specs=(
            P("cam", None, "tm"),
            P(None, "tm"),
            P(),
            P("tm", None, None),
            P(),
            P("cam", "tm"),
        ),
        out_specs=P("cam", "tm"),
        check_vma=False,
    )
```
